256 devices in a mesh: fsdp: 16 (over y, z_lo, core), uly: 4 (over x), blk: 4 (over z_hi).
Axes of the slice: x: 4, y: 4, z: 8 (z_hi: 4, z_lo: 2; z = z_hi * 2 + z_lo), core: 2. Of those that a mesh axis runs over, the one named last changes fastest.
Arguments:
- latents: bfloat16 [16, 3072, 3072], P('fsdp', ('uly', 'blk')), may hold values from -40 to 40
- sampler_noise: bfloat16 [16, 3072, 3072], P('fsdp', ('uly', 'blk')), may hold values from -6 to 6
- query_key_value_weight: bfloat16 [3, 3072, 1536], P(None, 'fsdp', 'uly'), may hold values from -0.375 to 0.375
- output_weight: bfloat16 [3072, 1536], P('fsdp', 'uly'), may hold values from -0.15625 to 0.15625
- adapter_down_map: bfloat16 [64, 1536], P(None, 'uly'), may hold values from -0.15625 to 0.15625
- adapter_up_map: bfloat16 [64, 3072], replicated, may hold values from -0.75 to 0.75
- valid_token_count: int32 [16], P('fsdp'), may hold values from 1536 to 3072
- advantage: float32 [16], P('fsdp'), may hold values from -3 to 3
- timestep_index: int32 [1], replicated, may hold values from 1 to 15
Outputs:
- next_latents: bfloat16 [16, 3072, 3072], P('fsdp', ('uly', 'blk'))
- log_ratio: float32 [16], P('fsdp')
- grad_down: float32 [64, 1536], P(None, 'uly')
- grad_up: float32 [64, 3072], replicated
The draws below stay inside these ranges and needn't reach their ends.
All inputs are finite; a program needn't handle non-finite values.
Results may differ from the reference program's by a relative error of at most 0.0055.
The reference program's roundings to bfloat16 on the way count: a program that leaves them out, or rounds other values in their place, can miss the bound.
Values may be sent and summed in bfloat16 or wider, within the bound.
No kernel may reach another device: no remote copies, remote signals or barrier semaphores. Data moves between devices by JAX's collectives and lax.ppermute only.
A program may use at most 128 MiB of HBM per device.

```python
import math
import jax
import jax.numpy as jnp
from jax import lax

MODEL_WIDTH = 3072
LOCAL_HEADS = 12
HEAD_SIZE = 128
ADAPTER_RANK = 64
STEPS = 16
VIDEOS = 16
SEQ = 3072


def draw_latents(key, part):
    base_key, row_key, col_key = jax.random.split(jax.random.fold_in(key, 21), 3)
    array_shape = (VIDEOS, SEQ, MODEL_WIDTH)
    row_scale = jnp.exp(jax.random.uniform(row_key, (VIDEOS, SEQ, 1), jnp.float32, math.log(0.3), math.log(3.0)))
    col_scale = jnp.exp(jax.random.uniform(col_key, (1, 1, MODEL_WIDTH), jnp.float32, math.log(0.3), math.log(3.0)))
    base = jax.random.normal(base_key, array_shape, jnp.float32)
    return jnp.clip(base * row_scale * col_scale, -40.0, 40.0).astype(jnp.bfloat16)


def draw_query_key_value_weight(key, part):
    base_key = jax.random.fold_in(jax.random.fold_in(key, 7), 0)
    width = LOCAL_HEADS * HEAD_SIZE
    spread = 1.6 / math.sqrt(MODEL_WIDTH)
    base = jax.random.normal(base_key, (3, MODEL_WIDTH, width), jnp.float32) * spread
    return jnp.clip(base, -0.375, 0.375).astype(jnp.bfloat16)


def touch_ends(values, key, least, largest):
    longest = values.shape.index(max(values.shape))
    spots = []
    for shift in (0, 1):
        where = [jax.random.randint(jax.random.fold_in(key, axis), (), 0, length) for axis, length in enumerate(values.shape)]
        where[longest] = (where[longest] + shift) % values.shape[longest]
        spots.append(tuple(where))
    return values.at[spots[0]].set(least).at[spots[1]].set(largest)


def shard_levels(key, dims, shards, smallest, largest):
    def one(axis_at, blocks):
        steps = jax.random.uniform(jax.random.fold_in(jax.random.fold_in(key, 6), axis_at), (blocks,), jnp.float32, smallest / len(shards), largest / len(shards))
        return jnp.repeat(jnp.exp(steps), dims[axis_at] // blocks).reshape((-1,) + (1,) * (len(dims) - axis_at - 1))

    level = one(*shards[0])
    for cut in shards[1:]:
        level = level * one(*cut)
    return level


def normal_values(rng, dims, scale, most, pieces=(), held_as=jnp.bfloat16):
    drawn = jax.random.normal(rng, dims, jnp.float32) * scale
    if len(pieces) > 0:
        drawn = shard_levels(rng, dims, pieces, -0.22, 0.18) * drawn
    return jnp.clip(drawn, min=-most, max=most).astype(held_as)


def setup_inputs(seed: int = 0) -> dict:
    key_of = jax.random.split(jax.random.key(seed), 10)
    latents = draw_latents(jax.random.fold_in(key_of[9], 71), 0)
    sampler_noise = normal_values(key_of[1], (VIDEOS, SEQ, MODEL_WIDTH), 1.0, 6.0, ((0, 16), (1, 16)))
    query_key_value_weight = draw_query_key_value_weight(jax.random.fold_in(key_of[9], 71), 0)
    output_weight = normal_values(key_of[3], (MODEL_WIDTH, LOCAL_HEADS * HEAD_SIZE), (LOCAL_HEADS * HEAD_SIZE) ** -0.5, 0.15625, ((0, 16), (1, 4)))
    adapter_down_map = normal_values(key_of[4], (ADAPTER_RANK, LOCAL_HEADS * HEAD_SIZE), (LOCAL_HEADS * HEAD_SIZE) ** -0.5, 0.15625, ((1, 4),))
    adapter_up_map = normal_values(key_of[5], (ADAPTER_RANK, MODEL_WIDTH), ADAPTER_RANK ** -0.5, 0.75)
    valid_token_count = touch_ends(jax.random.randint(key_of[6], (VIDEOS,), SEQ // 2, SEQ + 1), jax.random.fold_in(key_of[6], 1), SEQ // 2, SEQ).astype(jnp.int32)
    advantage = normal_values(key_of[7], (VIDEOS,), 1.0, 3.0, ((0, 16),), jnp.float32)
    timestep_index = jax.random.randint(key_of[8], (1,), 1, STEPS).astype(jnp.int32)
    return {"latents": latents, "sampler_noise": sampler_noise, "query_key_value_weight": query_key_value_weight, "output_weight": output_weight, "adapter_down_map": adapter_down_map, "adapter_up_map": adapter_up_map, "valid_token_count": valid_token_count, "advantage": advantage, "timestep_index": timestep_index}


noise_level = 0.7
loss_scale = 4194304.0
rms_eps = 1e-06

def reference(latents, sampler_noise, query_key_value_weight, output_weight, adapter_down_map, adapter_up_map, valid_token_count, advantage, timestep_index):
    step_float = timestep_index[0].astype(jnp.float32)
    time_now = 1.0 - step_float / STEPS
    step_size = 1.0 / STEPS
    noise_std = noise_level * jnp.sqrt(time_now / (1.0 - time_now))
    drift_gain = 1.0 + noise_level ** 2 / 2.0
    ratio_gain = jnp.sqrt(step_size) * drift_gain / noise_std
    positions = jnp.arange(SEQ, dtype=jnp.int32)

    def one_video(inputs):
        video_lat, video_noise, limit, video_adv = inputs
        current = video_lat.astype(jnp.float32)
        normed = (current * lax.rsqrt(lax.optimization_barrier(jnp.mean(current * current, -1, keepdims=True)) + rms_eps)).astype(jnp.bfloat16)
        query_all = jnp.dot(normed, query_key_value_weight[0], preferred_element_type=jnp.float32).astype(jnp.bfloat16)
        key_all = jnp.dot(normed, query_key_value_weight[1], preferred_element_type=jnp.float32).astype(jnp.bfloat16)
        value_all = jnp.dot(normed, query_key_value_weight[2], preferred_element_type=jnp.float32).astype(jnp.bfloat16)
        key_ok = positions < limit

        def head_attention(head_id):
            start = (head_id * HEAD_SIZE).astype(jnp.int32)
            query_head = lax.dynamic_slice_in_dim(query_all, start, HEAD_SIZE, 1)
            key_head = lax.dynamic_slice_in_dim(key_all, start, HEAD_SIZE, 1)
            value_head = lax.dynamic_slice_in_dim(value_all, start, HEAD_SIZE, 1)
            scores = jnp.dot(query_head, key_head.T, preferred_element_type=jnp.float32) * (1.0 / math.sqrt(HEAD_SIZE))
            masked = jnp.where(key_ok[None, :], scores, -1e+30)
            row_max = lax.optimization_barrier(jnp.max(masked, -1, keepdims=True))
            exp_terms = jnp.where(key_ok[None, :], jnp.exp(masked - row_max), 0.0)
            weights = (exp_terms / lax.optimization_barrier(jnp.sum(exp_terms, -1, keepdims=True))).astype(jnp.bfloat16)
            return jnp.dot(weights, value_head, preferred_element_type=jnp.float32).astype(jnp.bfloat16)
        per_head = lax.map(head_attention, jnp.arange(LOCAL_HEADS, dtype=jnp.int32))
        attention_output = jnp.transpose(per_head, (1, 0, 2)).reshape(SEQ, LOCAL_HEADS * HEAD_SIZE)
        velocity = jnp.dot(attention_output, output_weight.T, preferred_element_type=jnp.float32)
        narrow_projection = jnp.dot(attention_output, adapter_down_map.T, preferred_element_type=jnp.float32).astype(jnp.bfloat16)
        adapter_result = jnp.dot(narrow_projection, adapter_up_map, preferred_element_type=jnp.float32)
        noise_f = video_noise.astype(jnp.float32)
        moved = current - step_size * (drift_gain * velocity + noise_level ** 2 * current / (2.0 * (1.0 - time_now)))
        next_video = (moved + noise_std * jnp.sqrt(step_size) * noise_f).astype(jnp.bfloat16)
        standard = noise_f + ratio_gain * adapter_result
        tok_ok = key_ok[:, None]
        valid_len = limit.astype(jnp.float32)
        ratio_log = jnp.sum(jnp.where(tok_ok, noise_f * noise_f - standard * standard, 0.0)) / (2.0 * valid_len * MODEL_WIDTH)
        coef = loss_scale * video_adv * jnp.exp(ratio_log) * ratio_gain / (VIDEOS * valid_len * MODEL_WIDTH)
        delta_gradient = (jnp.where(tok_ok, standard, 0.0) * coef).astype(jnp.bfloat16)
        up_part = jnp.dot(narrow_projection.T, delta_gradient, preferred_element_type=jnp.float32)
        narrow_gradient = jnp.dot(delta_gradient, adapter_up_map.T, preferred_element_type=jnp.float32).astype(jnp.bfloat16)
        down_part = jnp.dot(narrow_gradient.T, attention_output, preferred_element_type=jnp.float32)
        return (next_video, ratio_log, down_part, up_part)
    next_latents, log_ratio, down_parts, up_parts = lax.map(one_video, (latents, sampler_noise, valid_token_count, advantage))
    return (next_latents, log_ratio, lax.optimization_barrier(jnp.sum(down_parts, 0)), lax.optimization_barrier(jnp.sum(up_parts, 0)))
```

```python
import functools
import math

import jax
import jax.numpy as jnp
from jax import lax
from jax.experimental import pallas as pl
from jax.experimental.pallas import tpu as pltpu
from jax.sharding import PartitionSpec as P

HEAD_SIZE = 128
STEPS = 16

noise_level = 0.7
loss_scale = 4194304.0
rms_eps = 1e-06


def shift(x, axis, step):
    n = lax.axis_size(axis)
    return lax.ppermute(x, axis, [(i, (i + step) % n) for i in range(n)])


def exchange(x, axis, mask):
    n = lax.axis_size(axis)
    return lax.ppermute(x, axis, [(i, i ^ mask) for i in range(n)])


def ring_gather(x, axis):
    half = x.shape[0] // 2
    first, second = x[:half], x[half:]
    left_first = shift(first, axis, 1)
    right_second = shift(second, axis, -1)
    far_first = shift(left_first, axis, 1)
    far_second = shift(right_second, axis, -1)
    left_second = shift(second, axis, 1)
    right_first = shift(first, axis, -1)
    return (left_first, left_second), (right_first, right_second), (far_first, far_second)


def four_sum(x, axis):
    return (x + exchange(x, axis, 1)) + (exchange(x, axis, 2) + exchange(x, axis, 3))


def attention_body(bases_ref, limit_ref, q_ref, *refs, seg_rows, seg_stride):
    out_ref = refs[-1]
    blocks = refs[:-1]
    limit = limit_ref[0]
    scale = math.log2(math.e) / math.sqrt(HEAD_SIZE)
    query = q_ref[...]
    scores = []
    top = None
    for at, ref in enumerate(blocks):
        rows = ref.shape[0]
        s = lax.dot_general(
            query, ref[:, :HEAD_SIZE], (((1,), (1,)), ((), ())), preferred_element_type=jnp.float32
        )
        parts = []
        row = lax.broadcasted_iota(jnp.int32, (1, seg_rows), 1)
        for seg in range(rows // seg_rows):
            base = bases_ref[at, seg]
            parts.append(jnp.where(row + base < limit, 0.0, -1e30))
        s = s + jnp.concatenate(parts, 1)
        most = jnp.max(s, -1, keepdims=True)
        top = most if top is None else jnp.maximum(top, most)
        scores.append(s)
    total = None
    acc = None
    for ref, s in zip(blocks, scores):
        p = jnp.exp2((s - top) * scale)
        part = jnp.sum(p, -1, keepdims=True)
        o = jnp.dot(
            p.astype(jnp.bfloat16), ref[:, HEAD_SIZE:], preferred_element_type=jnp.float32
        )
        total = part if total is None else total + part
        acc = o if acc is None else acc + o
    out_ref[...] = (acc / total).astype(jnp.bfloat16)


def attend(query_rows, head, blocks, bases, limit, seg_rows):
    rows = query_rows.shape[0]
    tile = 256
    return pl.pallas_call(
        functools.partial(attention_body, seg_rows=seg_rows, seg_stride=0),
        out_shape=jax.ShapeDtypeStruct((rows, HEAD_SIZE), jnp.bfloat16),
        grid=(rows // tile,),
        in_specs=[
            pl.BlockSpec(memory_space=pltpu.SMEM),
            pl.BlockSpec(memory_space=pltpu.SMEM),
            pl.BlockSpec((tile, HEAD_SIZE), lambda i: (i, head)),
        ]
        + [pl.BlockSpec(b.shape, lambda i: (0, 0)) for b in blocks],
        out_specs=pl.BlockSpec((tile, HEAD_SIZE), lambda i: (i, 0)),
        name="attend",
    )(bases, limit, query_rows, *blocks)


def shards(
    latents,
    sampler_noise,
    query_key_value_weight,
    output_weight,
    adapter_down_map,
    adapter_up_map,
    valid_token_count,
    advantage,
    timestep_index,
):
    uly_count = lax.axis_size("uly")
    blk_count = lax.axis_size("blk")
    fsdp_count = lax.axis_size("fsdp")
    uly_id = lax.axis_index("uly")
    blk_id = lax.axis_index("blk")
    fsdp_id = lax.axis_index("fsdp")
    core_id = fsdp_id % 2
    y_id = fsdp_id // 4
    limit = valid_token_count[0]

    current = latents[0].astype(jnp.float32)
    rows = current.shape[0]
    width = current.shape[1]
    normed = (current * lax.rsqrt(jnp.mean(current * current, -1, keepdims=True) + rms_eps)).astype(
        jnp.bfloat16
    )
    heads_here = query_key_value_weight.shape[2] // HEAD_SIZE
    local_columns = heads_here * HEAD_SIZE

    pieces = []
    for h in range(heads_here):
        cols = slice(h * HEAD_SIZE, (h + 1) * HEAD_SIZE)
        pieces += [query_key_value_weight[1][:, cols], query_key_value_weight[2][:, cols]]
    pieces.append(query_key_value_weight[0])
    weight_rows = lax.all_gather(jnp.concatenate(pieces, 1), "fsdp", axis=0, tiled=True)

    left, right, far = ring_gather(normed, "uly")
    gathered = jnp.concatenate((normed,) + left + right + far, 0)
    seg_shift = (0, -1, 1, 2)

    def head_owners(x):
        return jnp.concatenate(
            (x, shift(x, "uly", -1), shift(x, "uly", 1), shift(x, "uly", 2)), 1
        )

    weight_full = lax.all_gather(head_owners(output_weight), "fsdp", axis=0, tiled=True)
    down_full = head_owners(adapter_down_map)

    def product(x, w):
        return jnp.dot(x, w, preferred_element_type=jnp.float32).astype(jnp.bfloat16)

    pair = 2 * HEAD_SIZE
    key_values = [
        product(gathered, weight_rows[:, h * pair : (h + 1) * pair]) for h in range(heads_here)
    ]
    query_rows = product(gathered, weight_rows[:, heads_here * pair :])

    def base_of(blk_step, segs):
        b = (blk_id + blk_step) % blk_count
        return [(((uly_id + seg_shift[s]) % uly_count) * blk_count + b) * rows for s in segs]

    low, high = (0, 1), (2, 3)
    block_bases = [base_of(0, low) + base_of(0, high)]
    for step in (-1, 1, 2):
        for segs in (low, high):
            block_bases.append(base_of(step, segs) * 2)
    bases = jnp.stack([jnp.stack(b) for b in block_bases]).astype(jnp.int32)

    own_pieces = [[], [], [], []]
    for h in range(heads_here):
        left, right, far = ring_gather(key_values[h], "blk")
        out = attend(
            query_rows, h, (key_values[h],) + left + right + far, bases, valid_token_count, rows
        )
        seg = [out[s * rows : (s + 1) * rows] for s in range(4)]
        own_pieces[0].append(seg[0])
        own_pieces[1].append(shift(seg[1], "uly", -1))
        own_pieces[2].append(shift(seg[2], "uly", 1))
        own_pieces[3].append(shift(seg[3], "uly", 2))
    own_heads = jnp.concatenate([p for group in own_pieces for p in group], 1)

    contract_product = (((1,), (1,)), ((), ()))
    narrow_projection = lax.dot_general(
        own_heads, down_full, contract_product, preferred_element_type=jnp.float32
    ).astype(jnp.bfloat16)
    adapter_result = jnp.dot(narrow_projection, adapter_up_map, preferred_element_type=jnp.float32)
    step_float = timestep_index[0].astype(jnp.float32)
    time_now = 1.0 - step_float / STEPS
    step_size = 1.0 / STEPS
    noise_std = noise_level * jnp.sqrt(time_now / (1.0 - time_now))
    drift_gain = 1.0 + noise_level**2 / 2.0
    ratio_gain = jnp.sqrt(step_size) * drift_gain / noise_std
    noise_f = sampler_noise[0].astype(jnp.float32)
    standard = noise_f + ratio_gain * adapter_result
    tok_pos = (uly_id * blk_count + blk_id) * rows + jnp.arange(rows, dtype=jnp.int32)
    tok_ok = (tok_pos < limit)[:, None]
    valid_len = limit.astype(jnp.float32)
    partial_log = jnp.sum(jnp.where(tok_ok, noise_f * noise_f - standard * standard, 0.0)) / (
        2.0 * valid_len * width
    )
    log_tile = four_sum(jnp.full((8, 128), partial_log), "uly")
    log_tile = four_sum(log_tile, "blk")
    log_ratio = log_tile[0, 0]
    coef = (
        loss_scale
        * advantage[0]
        * jnp.exp(log_ratio)
        * ratio_gain
        / (fsdp_count * valid_len * width)
    )

    masked = jnp.where(tok_ok, standard, 0.0).astype(jnp.bfloat16)
    first_axis = (((0,), (0,)), ((), ()))
    up_part = lax.dot_general(
        narrow_projection, masked, first_axis, preferred_element_type=jnp.float32
    )
    narrow_gradient = lax.dot_general(
        masked, adapter_up_map, contract_product, preferred_element_type=jnp.float32
    ).astype(jnp.bfloat16)
    down_part = lax.dot_general(
        narrow_gradient, own_heads, first_axis, preferred_element_type=jnp.float32
    )

    up_columns = width // uly_count

    def share(step, seg):
        at = ((uly_id + step) % uly_count) * up_columns
        up = lax.dynamic_slice_in_dim(up_part, at, up_columns, 1)
        return jnp.concatenate((up, down_part[:, seg * local_columns : (seg + 1) * local_columns]), 1)

    summed = (share(0, 0) + shift(share(1, 1), "uly", 1)) + (
        shift(share(-1, 2), "uly", -1) + shift(share(2, 3), "uly", 2)
    )
    summed = summed * coef
    half = summed.shape[0] // 2
    mine = lax.dynamic_slice_in_dim(summed, core_id * half, half, 0)
    other = lax.dynamic_slice_in_dim(summed, (1 - core_id) * half, half, 0)
    summed = mine + exchange(other, "fsdp", 1)
    part = half // 4

    def y_part(k):
        return lax.dynamic_slice_in_dim(summed, ((y_id + k) % 4) * part, part, 0)

    summed = (y_part(0) + shift(y_part(1), "fsdp", 4)) + (
        shift(y_part(2), "fsdp", 8) + shift(y_part(3), "fsdp", 12)
    )
    zs = []
    for lo in (0, 2):
        got = []
        for hi in range(4):
            if lo == 0 and hi == 0:
                got.append(summed)
            else:
                got.append(
                    lax.ppermute(
                        summed,
                        ("fsdp", "blk"),
                        [
                            (f * blk_count + b, (f ^ lo) * blk_count + (b ^ hi))
                            for f in range(fsdp_count)
                            for b in range(blk_count)
                        ],
                    )
                )
        zs.append((got[0] + got[1]) + (got[2] + got[3]))
    summed = zs[0] + zs[1]

    def in_order(rel, at):
        twice = jnp.stack([rel[0], rel[3], rel[2], rel[1]] * 2)
        return lax.dynamic_slice_in_dim(twice, (4 - at) % 4, 4, 0)

    by_y = in_order([summed] + [shift(summed, "fsdp", 4 * k) for k in (1, 2, 3)], y_id)
    by_y = by_y.reshape(half, summed.shape[1])
    up_mine = by_y[:, :up_columns]
    down_mine = by_y[:, up_columns:]
    by_x = in_order([up_mine] + [shift(up_mine, "uly", k) for k in (1, 2, 3)], uly_id)
    up_mine = jnp.transpose(by_x, (1, 0, 2)).reshape(half, width)
    up_other = exchange(up_mine, "fsdp", 1)
    down_other = exchange(down_mine, "fsdp", 1)

    def both(mine, other):
        twice = jnp.concatenate((mine, other, mine), 0)
        return lax.dynamic_slice_in_dim(twice, core_id * half, 2 * half, 0)

    grad_up = both(up_mine, up_other)
    grad_down = both(down_mine, down_other)

    velocity = lax.dot_general(
        own_heads, weight_full, contract_product, preferred_element_type=jnp.float32
    )
    moved = current - step_size * (
        drift_gain * velocity + noise_level**2 * current / (2.0 * (1.0 - time_now))
    )
    next_latents = (moved + noise_std * jnp.sqrt(step_size) * noise_f).astype(jnp.bfloat16)[None]
    return (next_latents, jnp.reshape(log_ratio, (1,)), grad_down, grad_up)


def solution(mesh):
    placed = (
        P("fsdp", ("uly", "blk"), None),
        P("fsdp", ("uly", "blk"), None),
        P(None, "fsdp", "uly"),
        P("fsdp", "uly"),
        P(None, "uly"),
        P(),
        P("fsdp"),
        P("fsdp"),
        P(),
    )
    return jax.shard_map(
        shards,
        mesh=mesh,
        in_specs=placed,
        out_specs=(P("fsdp", ("uly", "blk"), None), P("fsdp"), P(None, "uly"), P()),
        check_vma=False,
    )
```

```python
import math

import jax
import jax.numpy as jnp
from jax import lax
from jax.experimental import pallas as pl
from jax.experimental.pallas import tpu as pltpu
from jax.sharding import PartitionSpec as P


HEAD_SIZE = 128
STEPS = 16

noise_level = 0.7
loss_scale = 4194304.0
rms_eps = 1e-06


def shift(x, axis, step):
    n = lax.axis_size(axis)
    return lax.ppermute(x, axis, [(i, (i + step) % n) for i in range(n)])


def exchange(x, axis, mask):
    n = lax.axis_size(axis)
    return lax.ppermute(x, axis, [(i, i ^ mask) for i in range(n)])


def after(x, *earlier):
    return lax.optimization_barrier((x,) + earlier)[0]


def first_hop(x, axis):
    half = x.shape[0] // 2
    return shift(x[:half], axis, 1), shift(x[half:], axis, -1)


def other_hops(x, hop, axis):
    half = x.shape[0] // 2
    left_first, right_second = hop
    far_first = shift(left_first, axis, 1)
    far_second = shift(right_second, axis, -1)
    x = after(x, left_first, right_second)
    left_second = shift(x[half:], axis, 1)
    right_first = shift(x[:half], axis, -1)
    return left_first, left_second, right_first, right_second, far_first, far_second


def four_sum(x, axis):
    return (x + exchange(x, axis, 1)) + (exchange(x, axis, 2) + exchange(x, axis, 3))


def attention_body(q_ref, bias_ref, *refs):
    blocks, out_ref, pairs_ref, scores_ref, acc_ref = refs[:-4], *refs[-4:]
    scale = math.log2(math.e) / math.sqrt(HEAD_SIZE)
    at = 0
    for ref in blocks:
        pairs_ref[at : at + ref.shape[0]] = ref[...]
        at += ref.shape[0]
    chunk = scores_ref.shape[2]
    count = scores_ref.shape[0]
    rows = q_ref.shape[0]

    def score(c, top):
        start = pl.multiple_of(c * chunk, chunk)
        s = lax.dot_general(
            q_ref[...],
            pairs_ref[pl.ds(start, chunk), :HEAD_SIZE],
            (((1,), (1,)), ((), ())),
            preferred_element_type=jnp.float32,
        )
        s = s + bias_ref[:, pl.ds(start, chunk)]
        scores_ref[c] = s
        for col in range(0, chunk, 128):
            top = jnp.maximum(top, s[:, col : col + 128])
        return top

    top = lax.fori_loop(0, count, score, jnp.full((rows, 128), -jnp.inf, jnp.float32))
    top = jnp.max(top, -1, keepdims=True) * scale
    acc_ref[...] = jnp.zeros_like(acc_ref)

    def collect(c, total):
        start = pl.multiple_of(c * chunk, chunk)
        p = jnp.exp2(scores_ref[c] * scale - top)
        for col in range(0, chunk, 128):
            total = total + p[:, col : col + 128]
        acc_ref[...] += jnp.dot(
            p.astype(jnp.bfloat16),
            pairs_ref[pl.ds(start, chunk), HEAD_SIZE:],
            preferred_element_type=jnp.float32,
        )
        return total

    total = lax.fori_loop(0, count, collect, jnp.zeros((rows, 128), jnp.float32))
    out_ref[...] = (acc_ref[...] / jnp.sum(total, -1, keepdims=True)).astype(jnp.bfloat16)


def attend(query_rows, head, blocks, bias):
    rows = query_rows.shape[0]
    keys = bias.shape[1]
    chunk = 256

    def spec(block_rows, place):
        return pl.BlockSpec((block_rows, 2 * HEAD_SIZE), lambda i: (place, 0))

    return pl.pallas_call(
        attention_body,
        out_shape=jax.ShapeDtypeStruct((rows, HEAD_SIZE), jnp.bfloat16),
        grid=(1,),
        in_specs=[
            pl.BlockSpec((rows, HEAD_SIZE), lambda i: (0, head)),
            pl.BlockSpec(bias.shape, lambda i: (0, 0)),
        ]
        + [spec(block_rows, place) for _, block_rows, place in blocks],
        out_specs=pl.BlockSpec((rows, HEAD_SIZE), lambda i: (0, 0)),
        scratch_shapes=[
            pltpu.VMEM((keys, 2 * HEAD_SIZE), jnp.bfloat16),
            pltpu.VMEM((keys // chunk, rows, chunk), jnp.float32),
            pltpu.VMEM((rows, HEAD_SIZE), jnp.float32),
        ],
        name="attend",
    )(query_rows, bias, *[array for array, _, _ in blocks])


def standard_body(ints_ref, gain_ref, down_ref, up_ref, noise_ref, *refs):
    pieces, own_ref, narrow_ref, masked_ref, log_ref = refs[:-4], *refs[-4:]
    rows, width = noise_ref.shape
    for at, ref in enumerate(pieces):
        own_ref[:, at * HEAD_SIZE : (at + 1) * HEAD_SIZE] = ref[...]
    narrow = lax.dot_general(
        own_ref[...], down_ref[...], (((1,), (1,)), ((), ())), preferred_element_type=jnp.float32
    ).astype(jnp.bfloat16)
    narrow_ref[...] = narrow
    position = ints_ref[0] + lax.broadcasted_iota(jnp.int32, (rows, 1), 0)
    keep = position < ints_ref[1]
    chunk = 512

    def step(c, total):
        start = pl.multiple_of(c * chunk, chunk)
        change = jnp.dot(
            narrow_ref[...], up_ref[:, pl.ds(start, chunk)], preferred_element_type=jnp.float32
        )
        noise = noise_ref[:, pl.ds(start, chunk)].astype(jnp.float32)
        standard = noise + gain_ref[0] * change
        masked_ref[:, pl.ds(start, chunk)] = jnp.where(keep, standard, 0.0).astype(jnp.bfloat16)
        terms = jnp.where(keep, noise * noise - standard * standard, 0.0)
        for col in range(0, chunk, 128):
            total = total + terms[:, col : col + 128]
        return total

    total = lax.fori_loop(0, width // chunk, step, jnp.zeros((rows, 128), jnp.float32))
    log_ref[...] = jnp.full(log_ref.shape, jnp.sum(total))


def products_body(ints_ref, narrow_ref, masked_ref, up_ref, own_ref, *outs):
    width = masked_ref.shape[1]
    count = len(outs)
    columns = width // count
    own_columns = own_ref.shape[1] // count
    first_axis = (((0,), (0,)), ((), ()))
    low_grad = lax.dot_general(
        masked_ref[...], up_ref[...], (((1,), (1,)), ((), ())), preferred_element_type=jnp.float32
    ).astype(jnp.bfloat16)
    down = lax.dot_general(
        low_grad, own_ref[...], first_axis, preferred_element_type=jnp.float32
    )
    for step, out in enumerate(outs):
        start = pl.multiple_of(lax.rem(ints_ref[0] + step, count) * columns, 128)
        out[:, :columns] = lax.dot_general(
            narrow_ref[...],
            masked_ref[:, pl.ds(start, columns)],
            first_axis,
            preferred_element_type=jnp.float32,
        )
        seg = (0, 1, 3, 2)[step]
        out[:, columns:] = down[:, seg * own_columns : (seg + 1) * own_columns]


def shards(
    latents,
    sampler_noise,
    query_key_value_weight,
    output_weight,
    adapter_down_map,
    adapter_up_map,
    valid_token_count,
    advantage,
    timestep_index,
):
    uly_count = lax.axis_size("uly")
    blk_count = lax.axis_size("blk")
    fsdp_count = lax.axis_size("fsdp")
    uly_id = lax.axis_index("uly")
    blk_id = lax.axis_index("blk")
    fsdp_id = lax.axis_index("fsdp")
    core_id = fsdp_id % 2
    y_id = fsdp_id // 4
    limit = valid_token_count[0]

    current = latents[0].astype(jnp.float32)
    rows = current.shape[0]
    width = current.shape[1]
    normed = (current * lax.rsqrt(jnp.mean(current * current, -1, keepdims=True) + rms_eps)).astype(
        jnp.bfloat16
    )
    heads_here = query_key_value_weight.shape[2] // HEAD_SIZE
    local_columns = heads_here * HEAD_SIZE

    pieces = []
    for h in range(heads_here):
        cols = slice(h * HEAD_SIZE, (h + 1) * HEAD_SIZE)
        pieces += [query_key_value_weight[1][:, cols], query_key_value_weight[2][:, cols]]
    pieces.append(query_key_value_weight[0])
    weight_rows = lax.all_gather(jnp.concatenate(pieces, 1), "fsdp", axis=0, tiled=True)

    blocks = other_hops(normed, first_hop(normed, "uly"), "uly")
    gathered = jnp.concatenate((normed,) + blocks, 0)

    def head_owners(x):
        return jnp.concatenate(
            (x, shift(x, "uly", -1), shift(x, "uly", 1), shift(x, "uly", 2)), 1
        )

    output_columns = head_owners(after(output_weight, blocks[4]))
    down_full = head_owners(after(adapter_down_map, blocks[4]))

    def product(x, w):
        return jnp.dot(x, w, preferred_element_type=jnp.float32).astype(jnp.bfloat16)

    pair = 2 * HEAD_SIZE
    key_values = []
    for h in range(heads_here):
        key_values.append(product(gathered, weight_rows[:, h * pair : (h + 1) * pair]))
    query_rows = product(gathered, weight_rows[:, heads_here * pair :])

    group_rows = uly_count * rows
    key_index = jnp.arange(blk_count * group_rows, dtype=jnp.int32)

    def place(j, axis_id):
        return (axis_id + jnp.where(j == 0, 0, jnp.where(j == 1, 3, j - 1))) % 4

    key_pos = (
        place(key_index % group_rows // rows, uly_id) * blk_count
        + place(key_index // group_rows, blk_id)
    ) * rows + key_index % rows
    bias = jnp.where(key_pos < limit, 0.0, -1e30).astype(jnp.float32)[None]

    half_rows = group_rows // 2
    up, down = [], []
    for wave in range(heads_here + 1):
        up_parts, down_parts = [], []
        if wave > 0:
            size = half_rows
            last = 0 if wave == 1 else 2
            up_parts.append(up[-1][last * size : (last + 1) * size])
            down_parts.append(down[-1][last * size : (last + 1) * size])
            up_parts.append(key_values[wave - 1][half_rows:])
            down_parts.append(key_values[wave - 1][:half_rows])
        if wave < heads_here:
            up_parts.append(key_values[wave][:half_rows])
            down_parts.append(key_values[wave][half_rows:])
        up.append(shift(jnp.concatenate(up_parts, 0), "blk", 1))
        down.append(shift(jnp.concatenate(down_parts, 0), "blk", -1))

    own_pieces = [[], [], [], []]
    for h in range(heads_here):
        first = 0 if h == 0 else 2
        blocks = (
            (key_values[h], group_rows, 0),
            (up[h], half_rows, first),
            (up[h + 1], half_rows, 1),
            (down[h + 1], half_rows, 1),
            (down[h], half_rows, first),
            (up[h + 1], half_rows, 0),
            (down[h + 1], half_rows, 0),
        )
        out = attend(query_rows, h, blocks, bias)
        seg = [out[s * rows : (s + 1) * rows] for s in range(4)]
        own_pieces[0].append(seg[0])
        own_pieces[1].append(shift(seg[1], "uly", -1))
        own_pieces[2].append(shift(seg[2], "uly", 1))
        own_pieces[3].append(shift(seg[3], "uly", 2))
    weight_full = lax.all_gather(
        after(output_columns, up[-2], down[-2]), "fsdp", axis=0, tiled=True
    )

    step_float = timestep_index[0].astype(jnp.float32)
    time_now = 1.0 - step_float / STEPS
    step_size = 1.0 / STEPS
    noise_std = noise_level * jnp.sqrt(time_now / (1.0 - time_now))
    drift_gain = 1.0 + noise_level**2 / 2.0
    ratio_gain = jnp.sqrt(step_size) * drift_gain / noise_std
    noise_f = sampler_noise[0].astype(jnp.float32)
    valid_len = limit.astype(jnp.float32)
    ints = jnp.stack([(uly_id * blk_count + blk_id) * rows, limit]).astype(jnp.int32)
    smem = pl.BlockSpec(memory_space=pltpu.SMEM)
    vmem = pl.BlockSpec(memory_space=pltpu.VMEM)
    pieces = [p for group in own_pieces for p in group]
    own_heads, narrow_projection, masked, log_tile = pl.pallas_call(
        standard_body,
        out_shape=(
            jax.ShapeDtypeStruct((rows, len(pieces) * HEAD_SIZE), jnp.bfloat16),
            jax.ShapeDtypeStruct((rows, adapter_up_map.shape[0]), jnp.bfloat16),
            jax.ShapeDtypeStruct((rows, width), jnp.bfloat16),
            jax.ShapeDtypeStruct((8, 128), jnp.float32),
        ),
        in_specs=[smem, smem] + [vmem] * (3 + len(pieces)),
        out_specs=(vmem,) * 4,
        name="standard",
    )(ints, jnp.reshape(ratio_gain, (1,)), down_full, adapter_up_map, sampler_noise[0], *pieces)
    log_tile = four_sum(four_sum(log_tile, "uly"), "blk")
    log_ratio = log_tile[0, 0] / (2.0 * valid_len * width)
    coef = (
        loss_scale
        * advantage[0]
        * jnp.exp(log_ratio)
        * ratio_gain
        / (fsdp_count * valid_len * width)
    )

    up_columns = width // uly_count
    shares = pl.pallas_call(
        products_body,
        out_shape=[
            jax.ShapeDtypeStruct((adapter_up_map.shape[0], up_columns + local_columns), jnp.float32)
        ]
        * uly_count,
        in_specs=[smem] + [vmem] * 4,
        out_specs=[vmem] * uly_count,
        name="products",
    )(jnp.reshape(uly_id, (1,)).astype(jnp.int32), narrow_projection, masked, adapter_up_map, own_heads)
    summed = (shares[0] + shift(shares[1], "uly", 1)) + (
        shift(shares[2], "uly", 2) + shift(shares[3], "uly", -1)
    )
    summed = summed * coef
    half = summed.shape[0] // 2
    mine = lax.dynamic_slice_in_dim(summed, core_id * half, half, 0)
    other = lax.dynamic_slice_in_dim(summed, (1 - core_id) * half, half, 0)
    summed = mine + exchange(other, "fsdp", 1)
    part = half // 4

    def y_part(k):
        return lax.dynamic_slice_in_dim(summed, ((y_id + k) % 4) * part, part, 0)

    summed = (y_part(0) + shift(y_part(1), "fsdp", 4)) + (
        shift(y_part(2), "fsdp", 8) + shift(y_part(3), "fsdp", 12)
    )
    summed = summed + exchange(summed, "fsdp", 2)
    summed = four_sum(summed, "blk")

    def in_order(rel, at):
        twice = jnp.stack([rel[0], rel[3], rel[2], rel[1]] * 2)
        return lax.dynamic_slice_in_dim(twice, (4 - at) % 4, 4, 0)

    parts = [shift(summed, "fsdp", 4 * k) for k in (1, 2, 3)]
    velocity = lax.dot_general(
        own_heads, weight_full, (((1,), (1,)), ((), ())), preferred_element_type=jnp.float32
    )
    moved = current - step_size * (
        drift_gain * velocity + noise_level**2 * current / (2.0 * (1.0 - time_now))
    )
    next_latents = (moved + noise_std * jnp.sqrt(step_size) * noise_f).astype(jnp.bfloat16)[None]
    next_latents, *parts = lax.optimization_barrier((next_latents, *parts))
    by_y = in_order([summed] + parts, y_id)
    by_y = by_y.reshape(half, summed.shape[1])
    up_mine = by_y[:, :up_columns]
    down_mine = by_y[:, up_columns:]
    by_x = in_order([up_mine] + [shift(up_mine, "uly", k) for k in (1, 2, 3)], uly_id)
    up_mine = jnp.transpose(by_x, (1, 0, 2)).reshape(half, width)
    up_other = exchange(up_mine, "fsdp", 1)
    down_other = exchange(down_mine, "fsdp", 1)

    def both(mine, other):
        twice = jnp.concatenate((mine, other, mine), 0)
        return lax.dynamic_slice_in_dim(twice, core_id * half, 2 * half, 0)

    grad_up = both(up_mine, up_other)
    grad_down = both(down_mine, down_other)

    return (next_latents, jnp.reshape(log_ratio, (1,)), grad_down, grad_up)


def solution(mesh):
    placed = (
        P("fsdp", ("uly", "blk"), None),
        P("fsdp", ("uly", "blk"), None),
        P(None, "fsdp", "uly"),
        P("fsdp", "uly"),
        P(None, "uly"),
        P(),
        P("fsdp"),
        P("fsdp"),
        P(),
    )

    return jax.shard_map(
        shards,
        mesh=mesh,
        in_specs=placed,
        out_specs=(P("fsdp", ("uly", "blk"), None), P("fsdp"), P(None, "uly"), P()),
        check_vma=False,
    )
```

```python
import math

import jax
import jax.numpy as jnp
from jax import lax
from jax.experimental import pallas as pl
from jax.experimental.pallas import tpu as pltpu
from jax.sharding import PartitionSpec as P


HEAD_SIZE = 128
STEPS = 16

noise_level = 0.7
loss_scale = 4194304.0
rms_eps = 1e-06


smem = pl.BlockSpec(memory_space=pltpu.SMEM)
vmem = pl.BlockSpec(memory_space=pltpu.VMEM)
last_axis = (((1,), (1,)), ((), ()))
first_axis = (((0,), (0,)), ((), ()))


def shift(x, axis, step):
    n = lax.axis_size(axis)
    return lax.ppermute(x, axis, [(i, (i + step) % n) for i in range(n)])


def exchange(x, axis, mask):
    n = lax.axis_size(axis)
    return lax.ppermute(x, axis, [(i, i ^ mask) for i in range(n)])


def after(x, *earlier):
    return lax.optimization_barrier((x,) + earlier)[0]


def four_sum(parts):
    return (parts[0] + parts[1]) + (parts[2] + parts[3])


def project_body(ints_ref, own_ref, left_ref, right_ref, up_ref, down_ref, w_ref, out_ref, all_ref):
    rows = own_ref.shape[0]
    half = rows // 2

    @pl.when(pl.program_id(0) == 0)
    def _():
        odd = lax.rem(ints_ref[0], 2)
        left = pl.multiple_of((3 - 2 * odd) * rows, half)
        right = pl.multiple_of((1 + 2 * odd) * rows, half)
        all_ref[:rows] = own_ref[...]
        all_ref[pl.ds(left, half)] = left_ref[...]
        all_ref[pl.ds(left + half, half)] = up_ref[half:]
        all_ref[pl.ds(right, half)] = down_ref[half:]
        all_ref[pl.ds(right + half, half)] = right_ref[...]
        all_ref[2 * rows : 2 * rows + half] = up_ref[:half]
        all_ref[2 * rows + half : 3 * rows] = down_ref[:half]

    out_ref[...] = jnp.dot(
        all_ref[...], w_ref[...], preferred_element_type=jnp.float32
    ).astype(jnp.bfloat16)


def query_body(all_ref, w_ref, out_ref):
    out_ref[...] = jnp.dot(
        all_ref[...], w_ref[...], preferred_element_type=jnp.float32
    ).astype(jnp.bfloat16)


def attention_body(q_ref, bias_ref, *refs):
    blocks, outs, (pairs_ref, scores_ref, acc_ref) = refs[:-7], refs[-7:-3], refs[-3:]
    scale = math.log2(math.e) / math.sqrt(HEAD_SIZE)
    at = 0
    for ref in blocks:
        pairs_ref[at : at + ref.shape[0]] = ref[...]
        at += ref.shape[0]
    chunk = scores_ref.shape[2]
    count = scores_ref.shape[0]
    rows = q_ref.shape[0]

    def score(c, top):
        start = pl.multiple_of(c * chunk, chunk)
        s = lax.dot_general(
            q_ref[...],
            pairs_ref[pl.ds(start, chunk), :HEAD_SIZE],
            last_axis,
            preferred_element_type=jnp.float32,
        )
        s = s + bias_ref[:, pl.ds(start, chunk)]
        scores_ref[c] = s
        for col in range(0, chunk, 128):
            top = jnp.maximum(top, s[:, col : col + 128])
        return top

    top = lax.fori_loop(0, count, score, jnp.full((rows, 128), -jnp.inf, jnp.float32))
    top = jnp.max(top, -1, keepdims=True) * scale
    acc_ref[...] = jnp.zeros_like(acc_ref)

    def collect(c, total):
        start = pl.multiple_of(c * chunk, chunk)
        p = jnp.exp2(scores_ref[c] * scale - top)
        for col in range(0, chunk, 128):
            total = total + p[:, col : col + 128]
        acc_ref[...] += jnp.dot(
            p.astype(jnp.bfloat16),
            pairs_ref[pl.ds(start, chunk), HEAD_SIZE:],
            preferred_element_type=jnp.float32,
        )
        return total

    total = lax.fori_loop(0, count, collect, jnp.zeros((rows, 128), jnp.float32))
    out = (acc_ref[...] / jnp.sum(total, -1, keepdims=True)).astype(jnp.bfloat16)
    seg = rows // len(outs)
    for k, ref in enumerate(outs):
        ref[...] = out[k * seg : (k + 1) * seg]


def attend(query_rows, first_head, heads, blocks, bias):
    rows = query_rows.shape[0]
    keys = bias.shape[1]
    seg = rows // 4
    chunk = 256

    def spec(array, place):
        return pl.BlockSpec((None,) + array.shape[1:], lambda i: (i + place, 0, 0))

    return pl.pallas_call(
        attention_body,
        out_shape=[jax.ShapeDtypeStruct((seg, heads * HEAD_SIZE), jnp.bfloat16)] * 4,
        grid=(heads,),
        in_specs=[
            pl.BlockSpec((rows, HEAD_SIZE), lambda i: (0, i + first_head)),
            pl.BlockSpec(bias.shape, lambda i: (0, 0)),
        ]
        + [spec(array, place) for array, place in blocks],
        out_specs=[pl.BlockSpec((seg, HEAD_SIZE), lambda i: (0, i))] * 4,
        scratch_shapes=[
            pltpu.VMEM((keys, 2 * HEAD_SIZE), jnp.bfloat16),
            pltpu.VMEM((keys // chunk, rows, chunk), jnp.float32),
            pltpu.VMEM((rows, HEAD_SIZE), jnp.float32),
        ],
        name="attend",
    )(query_rows, bias, *[array for array, _ in blocks])


def standard_body(ints_ref, gain_ref, down_ref, up_ref, noise_ref, *refs):
    pieces, own_ref, narrow_ref, masked_ref, log_ref = refs[:-4], *refs[-4:]
    rows, width = noise_ref.shape
    at = 0
    for ref in pieces:
        own_ref[:, at : at + ref.shape[1]] = ref[...]
        at += ref.shape[1]
    narrow = lax.dot_general(
        own_ref[...], down_ref[...], last_axis, preferred_element_type=jnp.float32
    ).astype(jnp.bfloat16)
    narrow_ref[...] = narrow
    position = ints_ref[0] + lax.broadcasted_iota(jnp.int32, (rows, 1), 0)
    keep = position < ints_ref[1]
    chunk = 512

    def step(c, total):
        start = pl.multiple_of(c * chunk, chunk)
        change = jnp.dot(
            narrow_ref[...], up_ref[:, pl.ds(start, chunk)], preferred_element_type=jnp.float32
        )
        noise = noise_ref[:, pl.ds(start, chunk)].astype(jnp.float32)
        standard = noise + gain_ref[0] * change
        masked_ref[:, pl.ds(start, chunk)] = jnp.where(keep, standard, 0.0).astype(jnp.bfloat16)
        terms = jnp.where(keep, noise * noise - standard * standard, 0.0)
        for col in range(0, chunk, 128):
            total = total + terms[:, col : col + 128]
        return total

    total = lax.fori_loop(0, width // chunk, step, jnp.zeros((rows, 128), jnp.float32))
    log_ref[...] = jnp.full(log_ref.shape, jnp.sum(total))


def products_body(ints_ref, narrow_ref, masked_ref, up_ref, own_ref, log_ref, *outs):
    width = masked_ref.shape[1]
    count = len(outs)
    columns = width // count
    own_columns = own_ref.shape[1] // count
    low_grad = lax.dot_general(
        masked_ref[...], up_ref[...], last_axis, preferred_element_type=jnp.float32
    ).astype(jnp.bfloat16)
    down = lax.dot_general(
        low_grad, own_ref[...], first_axis, preferred_element_type=jnp.float32
    )
    for k, out in enumerate(outs):
        start = pl.multiple_of(jnp.bitwise_xor(ints_ref[0], k) * columns, 128)
        out[:, :columns] = lax.dot_general(
            narrow_ref[...],
            masked_ref[:, pl.ds(start, columns)],
            first_axis,
            preferred_element_type=jnp.float32,
        )
        out[:, columns : columns + own_columns] = down[:, k * own_columns : (k + 1) * own_columns]
        out[:, columns + own_columns :] = jnp.broadcast_to(
            log_ref[:1], (out.shape[0], log_ref.shape[1])
        )


def rows_body(ints_ref, *refs):
    parts, up_ref, down_ref = refs[:-2], *refs[-2:]
    rows = parts[0].shape[0]
    columns = up_ref.shape[1]
    for k, ref in enumerate(parts):
        start = pl.multiple_of(jnp.bitwise_xor(ints_ref[0], k) * rows, 8)
        up_ref[pl.ds(start, rows)] = ref[:, :columns]
        down_ref[pl.ds(start, rows)] = ref[:, columns:]


def columns_body(ints_ref, *refs):
    parts, out_ref = refs[:-1], refs[-1]
    columns = parts[0].shape[1]
    for k, ref in enumerate(parts):
        start = pl.multiple_of(jnp.bitwise_xor(ints_ref[0], k) * columns, 128)
        out_ref[:, pl.ds(start, columns)] = ref[...]


def move_body(scalars_ref, own_ref, w_ref, latents_ref, noise_ref, out_ref):
    velocity = lax.dot_general(
        own_ref[...], w_ref[...], last_axis, preferred_element_type=jnp.float32
    )
    current = latents_ref[...].astype(jnp.float32)
    moved = current - scalars_ref[0] * (
        scalars_ref[1] * velocity + noise_level**2 * current / scalars_ref[2]
    )
    out_ref[...] = (moved + scalars_ref[3] * noise_ref[...].astype(jnp.float32)).astype(
        jnp.bfloat16
    )


def shards(
    latents,
    sampler_noise,
    query_key_value_weight,
    output_weight,
    adapter_down_map,
    adapter_up_map,
    valid_token_count,
    advantage,
    timestep_index,
):
    uly_count = lax.axis_size("uly")
    blk_count = lax.axis_size("blk")
    fsdp_count = lax.axis_size("fsdp")
    uly_id = lax.axis_index("uly")
    blk_id = lax.axis_index("blk")
    uly_int = jnp.reshape(uly_id, (1,)).astype(jnp.int32)
    blk_int = jnp.reshape(blk_id, (1,)).astype(jnp.int32)
    limit = valid_token_count[0]
    rank = adapter_down_map.shape[0]

    current = latents[0].astype(jnp.float32)
    rows = current.shape[0]
    width = current.shape[1]
    normed = (current * lax.rsqrt(jnp.mean(current * current, -1, keepdims=True) + rms_eps)).astype(
        jnp.bfloat16
    )
    heads_here = query_key_value_weight.shape[2] // HEAD_SIZE
    local_columns = heads_here * HEAD_SIZE
    pair = 2 * HEAD_SIZE
    group_rows = uly_count * rows

    pieces = []
    for h in range(heads_here):
        cols = slice(h * HEAD_SIZE, (h + 1) * HEAD_SIZE)
        pieces += [query_key_value_weight[1][:, cols], query_key_value_weight[2][:, cols]]
    pieces.append(query_key_value_weight[0])
    weight_rows = lax.all_gather(jnp.concatenate(pieces, 1), "fsdp", axis=0, tiled=True)

    half = rows // 2
    left = shift(normed[:half], "uly", 1)
    right = shift(normed[half:], "uly", -1)
    second, first, _, _ = lax.optimization_barrier((normed[half:], normed[:half], left, right))
    up = shift(jnp.concatenate((left, second), 0), "uly", 1)
    down = shift(jnp.concatenate((right, first), 0), "uly", -1)

    maps = after(jnp.concatenate((output_weight, adapter_down_map), 0), up, down)
    maps = jnp.concatenate([maps] + [exchange(maps, "uly", k) for k in (1, 2, 3)], 1)
    output_columns, down_full = maps[: output_weight.shape[0]], maps[output_weight.shape[0] :]

    key_values, gathered = pl.pallas_call(
        project_body,
        out_shape=(
            jax.ShapeDtypeStruct((heads_here, group_rows, pair), jnp.bfloat16),
            jax.ShapeDtypeStruct((group_rows, width), jnp.bfloat16),
        ),
        grid=(heads_here,),
        in_specs=[smem] + [vmem] * 5 + [pl.BlockSpec((width, pair), lambda h: (0, h))],
        out_specs=(
            pl.BlockSpec((None, group_rows, pair), lambda h: (h, 0, 0)),
            pl.BlockSpec((group_rows, width), lambda h: (0, 0)),
        ),
        name="project",
    )(uly_int, normed, left, right, up, down, weight_rows)
    query_rows = pl.pallas_call(
        query_body,
        out_shape=jax.ShapeDtypeStruct((group_rows, local_columns), jnp.bfloat16),
        grid=(1,),
        in_specs=[
            pl.BlockSpec((group_rows, width), lambda i: (0, 0)),
            pl.BlockSpec((width, local_columns), lambda i: (0, 2)),
        ],
        out_specs=pl.BlockSpec((group_rows, local_columns), lambda i: (0, 0)),
        name="query",
    )(gathered, weight_rows)

    key_index = jnp.arange(blk_count * group_rows, dtype=jnp.int32)
    step = key_index // group_rows
    key_blk = (blk_id + jnp.where(step == 0, 0, jnp.where(step == 1, 3, step - 1))) % blk_count
    key_pos = (
        (uly_id ^ (key_index % group_rows // rows)) * blk_count + key_blk
    ) * rows + key_index % rows
    bias = jnp.where(key_pos < limit, 0.0, -1e30).astype(jnp.float32)[None]

    middle = group_rows // 2
    firsts, seconds = key_values[:, :middle], key_values[:, middle:]
    lead = heads_here - 1

    def wave(up_part, down_part):
        up_part, down_part = lax.optimization_barrier((up_part, down_part))
        up_part = shift(up_part, "blk", 1)
        down_part = shift(down_part, "blk", -1)
        return up_part, down_part

    def join(*parts):
        return jnp.concatenate(parts, 0)

    up_0, down_0 = wave(firsts[:lead], seconds[:lead])
    up_1, down_1 = wave(
        join(up_0, seconds[:lead], firsts[lead:]), join(down_0, firsts[:lead], seconds[lead:])
    )
    up_2, down_2 = wave(
        join(up_1[2 * lead :], seconds[lead:]), join(down_1[2 * lead :], firsts[lead:])
    )
    weight_full = lax.all_gather(after(output_columns, up_1, down_1), "fsdp", axis=0, tiled=True)

    def others(segs):
        return [segs[0]] + [exchange(segs[k], "uly", k) for k in (1, 2, 3)]

    segs = attend(
        query_rows,
        0,
        lead,
        (
            (key_values, 0),
            (up_0, 0),
            (up_1, lead),
            (down_1, lead),
            (down_0, 0),
            (up_1, 0),
            (down_1, 0),
        ),
        bias,
    )
    lead_pieces = others(segs)
    segs = attend(
        query_rows,
        lead,
        1,
        (
            (key_values, lead),
            (up_1, 2 * lead),
            (up_2, 1),
            (down_2, 1),
            (down_1, 2 * lead),
            (up_2, 0),
            (down_2, 0),
        ),
        bias,
    )
    last_pieces = others(segs)

    step_float = timestep_index[0].astype(jnp.float32)
    time_now = 1.0 - step_float / STEPS
    step_size = 1.0 / STEPS
    noise_std = noise_level * jnp.sqrt(time_now / (1.0 - time_now))
    drift_gain = 1.0 + noise_level**2 / 2.0
    ratio_gain = jnp.sqrt(step_size) * drift_gain / noise_std
    valid_len = limit.astype(jnp.float32)
    ints = jnp.stack([(uly_id * blk_count + blk_id) * rows, limit]).astype(jnp.int32)
    pieces = [p for both in zip(lead_pieces, last_pieces) for p in both]
    own_heads, narrow_projection, masked, log_tile = pl.pallas_call(
        standard_body,
        out_shape=(
            jax.ShapeDtypeStruct((rows, uly_count * local_columns), jnp.bfloat16),
            jax.ShapeDtypeStruct((rows, rank), jnp.bfloat16),
            jax.ShapeDtypeStruct((rows, width), jnp.bfloat16),
            jax.ShapeDtypeStruct((8, 128), jnp.float32),
        ),
        in_specs=[smem, smem] + [vmem] * (3 + len(pieces)),
        out_specs=(vmem,) * 4,
        name="standard",
    )(ints, jnp.reshape(ratio_gain, (1,)), down_full, adapter_up_map, sampler_noise[0], *pieces)

    up_columns = width // uly_count
    share_columns = up_columns + local_columns
    shares = pl.pallas_call(
        products_body,
        out_shape=[jax.ShapeDtypeStruct((rank, share_columns + 128), jnp.float32)] * uly_count,
        in_specs=[smem] + [vmem] * 5,
        out_specs=[vmem] * uly_count,
        name="products",
    )(uly_int, narrow_projection, masked, adapter_up_map, own_heads, log_tile)

    summed = four_sum([shares[0]] + [exchange(shares[k], "uly", k) for k in (1, 2, 3)])
    part = rank // blk_count

    def rows_of(k):
        return lax.dynamic_slice_in_dim(summed, (blk_id ^ k) * part, part, 0)

    summed = four_sum([rows_of(0)] + [exchange(rows_of(k), "blk", k) for k in (1, 2, 3)])
    log_ratio = summed[0, share_columns] / (2.0 * valid_len * width)
    coef = (
        loss_scale
        * advantage[0]
        * jnp.exp(log_ratio)
        * ratio_gain
        / (fsdp_count * valid_len * width)
    )
    summed = summed[:, :share_columns] * coef
    for unit in (4, 1):
        summed = four_sum([summed] + [exchange(summed, "fsdp", unit * k) for k in (1, 2, 3)])

    tile = 512
    scalars = jnp.stack(
        [
            jnp.float32(step_size),
            jnp.float32(drift_gain),
            2.0 * (1.0 - time_now),
            noise_std * jnp.sqrt(step_size),
        ]
    )
    token_tile = pl.BlockSpec((rows, tile), lambda i: (0, i))
    next_latents = pl.pallas_call(
        move_body,
        out_shape=jax.ShapeDtypeStruct((rows, width), jnp.bfloat16),
        grid=(width // tile,),
        in_specs=[
            smem,
            pl.BlockSpec(own_heads.shape, lambda i: (0, 0)),
            pl.BlockSpec((tile, own_heads.shape[1]), lambda i: (i, 0)),
            token_tile,
            token_tile,
        ],
        out_specs=token_tile,
        name="move",
    )(scalars, own_heads, weight_full, latents[0], sampler_noise[0])
    parts = [exchange(summed, "blk", k) for k in (1, 2, 3)]
    next_latents, *parts = lax.optimization_barrier((next_latents, *parts))
    up_mine, grad_down = pl.pallas_call(
        rows_body,
        out_shape=(
            jax.ShapeDtypeStruct((rank, up_columns), jnp.float32),
            jax.ShapeDtypeStruct((rank, local_columns), jnp.float32),
        ),
        in_specs=[smem] + [vmem] * 4,
        out_specs=(vmem,) * 2,
        name="rows",
    )(blk_int, summed, *parts)
    grad_up = pl.pallas_call(
        columns_body,
        out_shape=jax.ShapeDtypeStruct((rank, width), jnp.float32),
        in_specs=[smem] + [vmem] * 4,
        out_specs=vmem,
        name="columns",
    )(uly_int, up_mine, *[exchange(up_mine, "uly", k) for k in (1, 2, 3)])
    return (next_latents[None], jnp.reshape(log_ratio, (1,)), grad_down, grad_up)


def solution(mesh):
    placed = (
        P("fsdp", ("uly", "blk"), None),
        P("fsdp", ("uly", "blk"), None),
        P(None, "fsdp", "uly"),
        P("fsdp", "uly"),
        P(None, "uly"),
        P(),
        P("fsdp"),
        P("fsdp"),
        P(),
    )

    return jax.shard_map(
        shards,
        mesh=mesh,
        in_specs=placed,
        out_specs=(P("fsdp", ("uly", "blk"), None), P("fsdp"), P(None, "uly"), P()),
        check_vma=False,
    )
```

```python
import math

import jax
import jax.numpy as jnp
from jax import lax
from jax.experimental import pallas as pl
from jax.experimental.pallas import tpu as pltpu
from jax.sharding import PartitionSpec as P


HEAD_SIZE = 128
STEPS = 16

noise_level = 0.7
loss_scale = 4194304.0
rms_eps = 1e-06


smem = pl.BlockSpec(memory_space=pltpu.SMEM)
vmem = pl.BlockSpec(memory_space=pltpu.VMEM)
last_axis = (((1,), (1,)), ((), ()))
first_axis = (((0,), (0,)), ((), ()))


PLACE = (0, 2, 1, 3)
SLOT = ((0, 2, 3, 1), (2, 0, 1, 3), (0, 2, 3, 1), (2, 0, 1, 3))
VIDEO = [PLACE.index(p) for p in range(4)]
BLOCK = [[SLOT[VIDEO[p]].index(q) for q in range(4)] for p in range(4)]


def worker(f, b):
    w = f % 4
    return f - w + SLOT[w][b], PLACE[w]


def gather_tokens(x):
    count = lax.axis_size("blk")
    pairs = []
    for f in range(lax.axis_size("fsdp")):
        for b in range(count):
            to_f, to_b = worker(f, b)
            pairs.append((f * count + b, to_f * count + to_b))
    return lax.ppermute(x, ("fsdp", "blk"), pairs)


def return_tokens(x, mask):
    blks, ulys = lax.axis_size("blk"), lax.axis_size("uly")
    pairs = []
    for f in range(lax.axis_size("fsdp")):
        for b in range(blks):
            to_f, to_b = worker(f, b)
            for u in range(ulys):
                pairs.append(
                    ((to_f * ulys + u) * blks + to_b, (f * ulys + (u ^ mask)) * blks + b)
                )
    return lax.ppermute(x, ("fsdp", "uly", "blk"), pairs)


def shift(x, axis, step):
    n = lax.axis_size(axis)
    return lax.ppermute(x, axis, [(i, (i + step) % n) for i in range(n)])


def exchange(x, axis, mask):
    n = lax.axis_size(axis)
    return lax.ppermute(x, axis, [(i, i ^ mask) for i in range(n)])


def after(x, *earlier):
    return lax.optimization_barrier((x,) + earlier)[0]


def four_sum(parts):
    return (parts[0] + parts[1]) + (parts[2] + parts[3])


def project_body(
    ints_ref, a_ref, b_ref, left_a_ref, right_a_ref, up_ref, right_b_ref, far_b_ref, w_ref,
    pairs_ref, query_ref, all_ref, acc_ref,
):
    half = a_ref.shape[0]
    rows = 2 * half

    @pl.when(pl.program_id(0) == 0)
    def _():
        odd = lax.rem(ints_ref[0], 2)
        left = pl.multiple_of((3 - 2 * odd) * rows, half)
        right = pl.multiple_of((1 + 2 * odd) * rows, half)
        all_ref[:half] = a_ref[...]
        all_ref[half:rows] = b_ref[...]
        all_ref[pl.ds(left, half)] = left_a_ref[...]
        all_ref[pl.ds(left + half, half)] = up_ref[half:]
        all_ref[pl.ds(right, half)] = right_a_ref[...]
        all_ref[pl.ds(right + half, half)] = right_b_ref[...]
        all_ref[2 * rows : 2 * rows + half] = up_ref[:half]
        all_ref[2 * rows + half : 3 * rows] = far_b_ref[...]

    acc_ref[...] = jnp.zeros_like(acc_ref)
    depth = 512

    def step(c, carry):
        start = pl.multiple_of(c * depth, depth)
        acc_ref[...] += jnp.dot(
            all_ref[:, pl.ds(start, depth)],
            w_ref[pl.ds(start, depth)],
            preferred_element_type=jnp.float32,
        )
        return carry

    lax.fori_loop(0, all_ref.shape[1] // depth, step, 0)
    query_ref[...] = acc_ref[:, :HEAD_SIZE].astype(jnp.bfloat16)
    pairs_ref[...] = acc_ref[:, HEAD_SIZE:].astype(jnp.bfloat16)


def attention_body(q_ref, bias_ref, *refs):
    blocks, outs, (pairs_ref, scores_ref, acc_ref) = refs[:-7], refs[-7:-3], refs[-3:]
    scale = math.log2(math.e) / math.sqrt(HEAD_SIZE)
    at = 0
    for ref in blocks:
        pairs_ref[at : at + ref.shape[0]] = ref[...]
        at += ref.shape[0]
    chunk = scores_ref.shape[2]
    count = scores_ref.shape[0]
    rows = q_ref.shape[0]

    def score(c, top):
        start = pl.multiple_of(c * chunk, chunk)
        s = lax.dot_general(
            q_ref[...],
            pairs_ref[pl.ds(start, chunk), :HEAD_SIZE],
            last_axis,
            preferred_element_type=jnp.float32,
        )
        s = s + bias_ref[:, pl.ds(start, chunk)]
        scores_ref[c] = s
        for col in range(0, chunk, 128):
            top = jnp.maximum(top, s[:, col : col + 128])
        return top

    top = lax.fori_loop(0, count, score, jnp.full((rows, 128), -jnp.inf, jnp.float32))
    top = jnp.max(top, -1, keepdims=True) * scale
    acc_ref[...] = jnp.zeros_like(acc_ref)

    def collect(c, total):
        start = pl.multiple_of(c * chunk, chunk)
        p = jnp.exp2(scores_ref[c] * scale - top)
        for col in range(0, chunk, 128):
            total = total + p[:, col : col + 128]
        acc_ref[...] += jnp.dot(
            p.astype(jnp.bfloat16),
            pairs_ref[pl.ds(start, chunk), HEAD_SIZE:],
            preferred_element_type=jnp.float32,
        )
        return total

    total = lax.fori_loop(0, count, collect, jnp.zeros((rows, 128), jnp.float32))
    out = (acc_ref[...] / jnp.sum(total, -1, keepdims=True)).astype(jnp.bfloat16)
    seg = rows // len(outs)
    for k, ref in enumerate(outs):
        ref[...] = out[k * seg : (k + 1) * seg]


def attend(query_rows, first_head, heads, blocks, bias):
    rows = query_rows.shape[1]
    keys = bias.shape[1]
    seg = rows // 4
    chunk = 512

    def spec(array, place):
        return pl.BlockSpec((None,) + array.shape[1:], lambda i: (i + place, 0, 0))

    return pl.pallas_call(
        attention_body,
        out_shape=[jax.ShapeDtypeStruct((seg, heads * HEAD_SIZE), jnp.bfloat16)] * 4,
        grid=(heads,),
        in_specs=[
            pl.BlockSpec((None, rows, HEAD_SIZE), lambda i: (i + first_head, 0, 0)),
            pl.BlockSpec(bias.shape, lambda i: (0, 0)),
        ]
        + [spec(array, place) for array, place in blocks],
        out_specs=[pl.BlockSpec((seg, HEAD_SIZE), lambda i: (0, i))] * 4,
        scratch_shapes=[
            pltpu.VMEM((keys, 2 * HEAD_SIZE), jnp.bfloat16),
            pltpu.VMEM((keys // chunk, rows, chunk), jnp.float32),
            pltpu.VMEM((rows, HEAD_SIZE), jnp.float32),
        ],
        name="attend",
    )(query_rows, bias, *[array for array, _ in blocks])


def standard_body(ints_ref, gain_ref, down_ref, up_ref, noise_ref, *refs):
    pieces, own_ref, narrow_ref, masked_ref, log_ref = refs[:-4], *refs[-4:]
    rows, width = noise_ref.shape
    at = 0
    for ref in pieces:
        own_ref[:, at : at + ref.shape[1]] = ref[...]
        at += ref.shape[1]
    narrow = lax.dot_general(
        own_ref[...], down_ref[...], last_axis, preferred_element_type=jnp.float32
    ).astype(jnp.bfloat16)
    narrow_ref[...] = narrow
    position = ints_ref[0] + lax.broadcasted_iota(jnp.int32, (rows, 1), 0)
    keep = position < ints_ref[1]
    chunk = 512

    def step(c, total):
        start = pl.multiple_of(c * chunk, chunk)
        change = jnp.dot(
            narrow_ref[...], up_ref[:, pl.ds(start, chunk)], preferred_element_type=jnp.float32
        )
        noise = noise_ref[:, pl.ds(start, chunk)].astype(jnp.float32)
        standard = noise + gain_ref[0] * change
        masked_ref[:, pl.ds(start, chunk)] = jnp.where(keep, standard, 0.0).astype(jnp.bfloat16)
        terms = jnp.where(keep, noise * noise - standard * standard, 0.0)
        for col in range(0, chunk, 128):
            total = total + terms[:, col : col + 128]
        return total

    total = lax.fori_loop(0, width // chunk, step, jnp.zeros((rows, 128), jnp.float32))
    log_ref[...] = jnp.full(log_ref.shape, jnp.sum(total))


def products_body(ints_ref, narrow_ref, masked_ref, up_ref, own_ref, log_ref, *outs):
    width = masked_ref.shape[1]
    count = len(outs)
    columns = width // count
    own_columns = own_ref.shape[1] // count
    low_grad = lax.dot_general(
        masked_ref[...], up_ref[...], last_axis, preferred_element_type=jnp.float32
    ).astype(jnp.bfloat16)
    down = lax.dot_general(
        low_grad, own_ref[...], first_axis, preferred_element_type=jnp.float32
    )
    for k, out in enumerate(outs):
        start = pl.multiple_of(jnp.bitwise_xor(ints_ref[0], k) * columns, 128)
        out[:, :columns] = lax.dot_general(
            narrow_ref[...],
            masked_ref[:, pl.ds(start, columns)],
            first_axis,
            preferred_element_type=jnp.float32,
        )
        out[:, columns : columns + own_columns] = down[:, k * own_columns : (k + 1) * own_columns]
        out[:, columns + own_columns :] = jnp.broadcast_to(
            log_ref[:1], (out.shape[0], log_ref.shape[1])
        )


def rows_body(ints_ref, *refs):
    parts, up_ref, down_ref = refs[:-2], *refs[-2:]
    rows = parts[0].shape[0]
    columns = up_ref.shape[1]
    for k, ref in enumerate(parts):
        start = pl.multiple_of(jnp.bitwise_xor(ints_ref[0], k) * rows, 8)
        up_ref[pl.ds(start, rows)] = ref[:, :columns]
        down_ref[pl.ds(start, rows)] = ref[:, columns:]


def columns_body(ints_ref, *refs):
    parts, out_ref = refs[:-1], refs[-1]
    columns = parts[0].shape[1]
    for k, ref in enumerate(parts):
        start = pl.multiple_of(jnp.bitwise_xor(ints_ref[0], k) * columns, 128)
        out_ref[:, pl.ds(start, columns)] = ref[...]


def move_body(scalars_ref, own_ref, w_ref, latents_ref, noise_ref, out_ref):
    velocity = lax.dot_general(
        own_ref[...], w_ref[...], last_axis, preferred_element_type=jnp.float32
    )
    current = latents_ref[...].astype(jnp.float32)
    moved = current - scalars_ref[0] * (
        scalars_ref[1] * velocity + noise_level**2 * current / scalars_ref[2]
    )
    out_ref[...] = (moved + scalars_ref[3] * noise_ref[...].astype(jnp.float32)).astype(
        jnp.bfloat16
    )


def shards(
    latents,
    sampler_noise,
    query_key_value_weight,
    output_weight,
    adapter_down_map,
    adapter_up_map,
    valid_token_count,
    advantage,
    timestep_index,
):
    uly_count = lax.axis_size("uly")
    blk_count = lax.axis_size("blk")
    fsdp_count = lax.axis_size("fsdp")
    uly_id = lax.axis_index("uly")
    blk_id = lax.axis_index("blk")
    uly_int = jnp.reshape(uly_id, (1,)).astype(jnp.int32)
    blk_int = jnp.reshape(blk_id, (1,)).astype(jnp.int32)
    limit = valid_token_count[0]
    rank = adapter_down_map.shape[0]

    rows, width = latents.shape[1:]
    half = rows // 2
    video_slot = lax.axis_index("fsdp") % 4
    moved_a = gather_tokens(latents[0, :half])
    moved_b = gather_tokens(after(latents[0, half:], moved_a))
    work_limit = gather_tokens(jnp.full((8, 128), limit, jnp.int32))[0, 0]

    def norm(x):
        x = x.astype(jnp.float32)
        return (x * lax.rsqrt(jnp.mean(x * x, -1, keepdims=True) + rms_eps)).astype(jnp.bfloat16)

    normed_a, normed_b = norm(moved_a), norm(moved_b)
    heads_here = query_key_value_weight.shape[2] // HEAD_SIZE
    local_columns = heads_here * HEAD_SIZE
    pair = 2 * HEAD_SIZE
    group_rows = uly_count * rows

    weight = jnp.concatenate(
        [
            query_key_value_weight[j, :, h * HEAD_SIZE : (h + 1) * HEAD_SIZE]
            for h in range(heads_here)
            for j in range(3)
        ],
        1,
    )
    weight_rows = lax.all_gather(weight, "fsdp", axis=0, tiled=True)

    left_a = shift(normed_a, "uly", 1)
    right_a = shift(normed_a, "uly", -1)
    normed_b, relay, _ = lax.optimization_barrier((normed_b, left_a, right_a))
    up = shift(jnp.concatenate((relay, normed_b), 0), "uly", 1)
    right_b = shift(normed_b, "uly", -1)
    far_b = shift(right_b, "uly", -1)

    maps = after(jnp.concatenate((output_weight, adapter_down_map), 0), up, far_b)
    maps = jnp.concatenate([maps] + [exchange(maps, "uly", k) for k in (1, 2, 3)], 1)
    output_columns, down_full = maps[: output_weight.shape[0]], maps[output_weight.shape[0] :]

    key_values, query_rows = pl.pallas_call(
        project_body,
        out_shape=(
            jax.ShapeDtypeStruct((heads_here, group_rows, pair), jnp.bfloat16),
            jax.ShapeDtypeStruct((heads_here, group_rows, HEAD_SIZE), jnp.bfloat16),
        ),
        grid=(heads_here,),
        in_specs=[smem] + [vmem] * 7 + [pl.BlockSpec((width, local_columns), lambda h: (0, h))],
        out_specs=(
            pl.BlockSpec((None, group_rows, pair), lambda h: (h, 0, 0)),
            pl.BlockSpec((None, group_rows, HEAD_SIZE), lambda h: (h, 0, 0)),
        ),
        scratch_shapes=[
            pltpu.VMEM((group_rows, width), jnp.bfloat16),
            pltpu.VMEM((group_rows, local_columns), jnp.float32),
        ],
        name="project",
    )(uly_int, normed_a, normed_b, left_a, right_a, up, right_b, far_b, weight_rows)

    key_index = jnp.arange(blk_count * group_rows, dtype=jnp.int32)
    key_blk = jnp.array(BLOCK, jnp.int32)[blk_id]
    key_blk = jnp.stack([key_blk[video_slot ^ k] for k in range(4)])
    key_pos = (
        (uly_id ^ (key_index % group_rows // rows)) * blk_count
        + jnp.repeat(key_blk, group_rows)
    ) * rows + key_index % rows
    bias = jnp.where(key_pos < work_limit, 0.0, -1e30).astype(jnp.float32)[None]

    lead = heads_here - 1
    core = exchange(key_values, "fsdp", 1)
    chip_lead = exchange(key_values[:lead], "fsdp", 2)
    chip_last = exchange(after(key_values[lead:], chip_lead), "fsdp", 2)
    far_lead = exchange(chip_lead, "fsdp", 1)
    far_last = exchange(chip_last, "fsdp", 1)
    weight_full = lax.all_gather(after(output_columns, chip_last), "fsdp", axis=0, tiled=True)

    def others(segs):
        return [return_tokens(segs[k], k) for k in range(4)]

    segs = attend(
        query_rows, 0, lead, ((key_values, 0), (core, 0), (chip_lead, 0), (far_lead, 0)), bias
    )
    lead_pieces = others(segs)
    segs = attend(
        query_rows,
        lead,
        1,
        ((key_values, lead), (core, lead), (chip_last, 0), (far_last, 0)),
        bias,
    )
    last_pieces = others(segs)

    step_float = timestep_index[0].astype(jnp.float32)
    time_now = 1.0 - step_float / STEPS
    step_size = 1.0 / STEPS
    noise_std = noise_level * jnp.sqrt(time_now / (1.0 - time_now))
    drift_gain = 1.0 + noise_level**2 / 2.0
    ratio_gain = jnp.sqrt(step_size) * drift_gain / noise_std
    valid_len = limit.astype(jnp.float32)
    ints = jnp.stack([(uly_id * blk_count + blk_id) * rows, limit]).astype(jnp.int32)
    pieces = [p for both in zip(lead_pieces, last_pieces) for p in both]
    own_heads, narrow_projection, masked, log_tile = pl.pallas_call(
        standard_body,
        out_shape=(
            jax.ShapeDtypeStruct((rows, uly_count * local_columns), jnp.bfloat16),
            jax.ShapeDtypeStruct((rows, rank), jnp.bfloat16),
            jax.ShapeDtypeStruct((rows, width), jnp.bfloat16),
            jax.ShapeDtypeStruct((8, 128), jnp.float32),
        ),
        in_specs=[smem, smem] + [vmem] * (3 + len(pieces)),
        out_specs=(vmem,) * 4,
        name="standard",
    )(ints, jnp.reshape(ratio_gain, (1,)), down_full, adapter_up_map, sampler_noise[0], *pieces)

    up_columns = width // uly_count
    share_columns = up_columns + local_columns
    shares = pl.pallas_call(
        products_body,
        out_shape=[jax.ShapeDtypeStruct((rank, share_columns + 128), jnp.float32)] * uly_count,
        in_specs=[smem] + [vmem] * 5,
        out_specs=[vmem] * uly_count,
        name="products",
    )(uly_int, narrow_projection, masked, adapter_up_map, own_heads, log_tile)

    summed = four_sum([shares[0]] + [exchange(shares[k], "uly", k) for k in (1, 2, 3)])
    part = rank // blk_count

    def rows_of(k):
        return lax.dynamic_slice_in_dim(summed, (blk_id ^ k) * part, part, 0)

    summed = four_sum([rows_of(0)] + [exchange(rows_of(k), "blk", k) for k in (1, 2, 3)])
    log_ratio = summed[0, share_columns] / (2.0 * valid_len * width)
    coef = (
        loss_scale
        * advantage[0]
        * jnp.exp(log_ratio)
        * ratio_gain
        / (fsdp_count * valid_len * width)
    )
    summed = summed[:, :share_columns] * coef
    for unit in (4, 1):
        summed = four_sum([summed] + [exchange(summed, "fsdp", unit * k) for k in (1, 2, 3)])

    tile = 512
    scalars = jnp.stack(
        [
            jnp.float32(step_size),
            jnp.float32(drift_gain),
            2.0 * (1.0 - time_now),
            noise_std * jnp.sqrt(step_size),
        ]
    )
    token_tile = pl.BlockSpec((rows, tile), lambda i: (0, i))
    next_latents = pl.pallas_call(
        move_body,
        out_shape=jax.ShapeDtypeStruct((rows, width), jnp.bfloat16),
        grid=(width // tile,),
        in_specs=[
            smem,
            pl.BlockSpec(own_heads.shape, lambda i: (0, 0)),
            pl.BlockSpec((tile, own_heads.shape[1]), lambda i: (i, 0)),
            token_tile,
            token_tile,
        ],
        out_specs=token_tile,
        name="move",
    )(scalars, own_heads, weight_full, latents[0], sampler_noise[0])
    parts = [exchange(summed, "blk", k) for k in (1, 2, 3)]
    next_latents, *parts = lax.optimization_barrier((next_latents, *parts))
    up_mine, grad_down = pl.pallas_call(
        rows_body,
        out_shape=(
            jax.ShapeDtypeStruct((rank, up_columns), jnp.float32),
            jax.ShapeDtypeStruct((rank, local_columns), jnp.float32),
        ),
        in_specs=[smem] + [vmem] * 4,
        out_specs=(vmem,) * 2,
        name="rows",
    )(blk_int, summed, *parts)
    grad_up = pl.pallas_call(
        columns_body,
        out_shape=jax.ShapeDtypeStruct((rank, width), jnp.float32),
        in_specs=[smem] + [vmem] * 4,
        out_specs=vmem,
        name="columns",
    )(uly_int, up_mine, *[exchange(up_mine, "uly", k) for k in (1, 2, 3)])
    return (next_latents[None], jnp.reshape(log_ratio, (1,)), grad_down, grad_up)


def solution(mesh):
    placed = (
        P("fsdp", ("uly", "blk"), None),
        P("fsdp", ("uly", "blk"), None),
        P(None, "fsdp", "uly"),
        P("fsdp", "uly"),
        P(None, "uly"),
        P(),
        P("fsdp"),
        P("fsdp"),
        P(),
    )

    return jax.shard_map(
        shards,
        mesh=mesh,
        in_specs=placed,
        out_specs=(P("fsdp", ("uly", "blk"), None), P("fsdp"), P(None, "uly"), P()),
        check_vma=False,
    )
```

```python
import math

import jax
import jax.numpy as jnp
from jax import lax
from jax.experimental import pallas as pl
from jax.experimental.pallas import tpu as pltpu
from jax.sharding import PartitionSpec as P


HEAD_SIZE = 128
STEPS = 16

noise_level = 0.7
loss_scale = 4194304.0
rms_eps = 1e-06


smem = pl.BlockSpec(memory_space=pltpu.SMEM)
vmem = pl.BlockSpec(memory_space=pltpu.VMEM)
last_axis = (((1,), (1,)), ((), ()))
first_axis = (((0,), (0,)), ((), ()))


PLACE = (0, 2, 1, 3)
SLOT = ((0, 2, 3, 1), (2, 0, 1, 3), (0, 2, 3, 1), (2, 0, 1, 3))
VIDEO = [PLACE.index(p) for p in range(4)]
BLOCK = [[SLOT[VIDEO[p]].index(q) for q in range(4)] for p in range(4)]


def worker(f, b):
    w = f % 4
    return f - w + SLOT[w][b], PLACE[w]


def gather_tokens(x):
    count = lax.axis_size("blk")
    pairs = []
    for f in range(lax.axis_size("fsdp")):
        for b in range(count):
            to_f, to_b = worker(f, b)
            pairs.append((f * count + b, to_f * count + to_b))
    return lax.ppermute(x, ("fsdp", "blk"), pairs)


def return_tokens(x, mask):
    blks, ulys = lax.axis_size("blk"), lax.axis_size("uly")
    pairs = []
    for f in range(lax.axis_size("fsdp")):
        for b in range(blks):
            to_f, to_b = worker(f, b)
            for u in range(ulys):
                pairs.append(
                    ((to_f * ulys + u) * blks + to_b, (f * ulys + (u ^ mask)) * blks + b)
                )
    return lax.ppermute(x, ("fsdp", "uly", "blk"), pairs)


def shift(x, axis, step):
    n = lax.axis_size(axis)
    return lax.ppermute(x, axis, [(i, (i + step) % n) for i in range(n)])


def exchange(x, axis, mask):
    n = lax.axis_size(axis)
    return lax.ppermute(x, axis, [(i, i ^ mask) for i in range(n)])


def after(x, *earlier):
    return lax.optimization_barrier((x,) + earlier)[0]


def four_sum(parts):
    return (parts[0] + parts[1]) + (parts[2] + parts[3])


def arrange_body(w_ref, out_ref):
    at = 0
    for start in range(0, w_ref.shape[2], HEAD_SIZE):
        for j in range(3):
            out_ref[:, at : at + HEAD_SIZE] = w_ref[j, :, start : start + HEAD_SIZE]
            at += HEAD_SIZE


def project_body(
    ints_ref, a_ref, b_ref, left_a_ref, right_a_ref, up_ref, right_b_ref, far_b_ref, w_ref,
    pairs_ref, query_ref, all_ref,
):
    half = a_ref.shape[0]
    rows = 2 * half

    @pl.when(pl.program_id(0) == 0)
    def _():
        odd = lax.rem(ints_ref[0], 2)
        left = pl.multiple_of((3 - 2 * odd) * rows, half)
        right = pl.multiple_of((1 + 2 * odd) * rows, half)
        all_ref[:half] = a_ref[...]
        all_ref[half:rows] = b_ref[...]
        all_ref[pl.ds(left, half)] = left_a_ref[...]
        all_ref[pl.ds(left + half, half)] = up_ref[half:]
        all_ref[pl.ds(right, half)] = right_a_ref[...]
        all_ref[pl.ds(right + half, half)] = right_b_ref[...]
        all_ref[2 * rows : 2 * rows + half] = up_ref[:half]
        all_ref[2 * rows + half : 3 * rows] = far_b_ref[...]

    tile = 384

    def step(r, carry):
        start = pl.multiple_of(r * tile, tile)
        out = jnp.dot(
            all_ref[pl.ds(start, tile)], w_ref[...], preferred_element_type=jnp.float32
        ).astype(jnp.bfloat16)
        query_ref[pl.ds(start, tile)] = out[:, :HEAD_SIZE]
        pairs_ref[pl.ds(start, tile)] = out[:, HEAD_SIZE:]
        return carry

    lax.fori_loop(0, all_ref.shape[0] // tile, step, 0)


def attention_body(q_ref, bias_ref, *refs):
    blocks, outs, (pairs_ref, scores_ref, acc_ref) = refs[:-7], refs[-7:-3], refs[-3:]
    scale = math.log2(math.e) / math.sqrt(HEAD_SIZE)
    at = 0
    for ref in blocks:
        pairs_ref[at : at + ref.shape[0]] = ref[...]
        at += ref.shape[0]
    chunk = scores_ref.shape[2]
    count = scores_ref.shape[0]
    rows = q_ref.shape[0]

    def score(c, top):
        start = pl.multiple_of(c * chunk, chunk)
        s = lax.dot_general(
            q_ref[...],
            pairs_ref[pl.ds(start, chunk), :HEAD_SIZE],
            last_axis,
            preferred_element_type=jnp.float32,
        )
        s = s + bias_ref[:, pl.ds(start, chunk)]
        scores_ref[c] = s
        for col in range(0, chunk, 128):
            top = jnp.maximum(top, s[:, col : col + 128])
        return top

    top = lax.fori_loop(0, count, score, jnp.full((rows, 128), -jnp.inf, jnp.float32))
    top = jnp.max(top, -1, keepdims=True) * scale
    acc_ref[...] = jnp.zeros_like(acc_ref)

    def collect(c, total):
        start = pl.multiple_of(c * chunk, chunk)
        p = jnp.exp2(scores_ref[c] * scale - top)
        for col in range(0, chunk, 128):
            total = total + p[:, col : col + 128]
        acc_ref[...] += jnp.dot(
            p.astype(jnp.bfloat16),
            pairs_ref[pl.ds(start, chunk), HEAD_SIZE:],
            preferred_element_type=jnp.float32,
        )
        return total

    total = lax.fori_loop(0, count, collect, jnp.zeros((rows, 128), jnp.float32))
    out = (acc_ref[...] / jnp.sum(total, -1, keepdims=True)).astype(jnp.bfloat16)
    seg = rows // len(outs)
    for k, ref in enumerate(outs):
        ref[...] = out[k * seg : (k + 1) * seg]


def attend(query_rows, first_head, heads, blocks, bias):
    rows = query_rows.shape[1]
    keys = bias.shape[1]
    seg = rows // 4
    chunk = 512

    def spec(array, place):
        return pl.BlockSpec((None,) + array.shape[1:], lambda i: (i + place, 0, 0))

    return pl.pallas_call(
        attention_body,
        out_shape=[jax.ShapeDtypeStruct((seg, heads * HEAD_SIZE), jnp.bfloat16)] * 4,
        grid=(heads,),
        in_specs=[
            pl.BlockSpec((None, rows, HEAD_SIZE), lambda i: (i + first_head, 0, 0)),
            pl.BlockSpec(bias.shape, lambda i: (0, 0)),
        ]
        + [spec(array, place) for array, place in blocks],
        out_specs=[pl.BlockSpec((seg, HEAD_SIZE), lambda i: (0, i))] * 4,
        scratch_shapes=[
            pltpu.VMEM((keys, 2 * HEAD_SIZE), jnp.bfloat16),
            pltpu.VMEM((keys // chunk, rows, chunk), jnp.float32),
            pltpu.VMEM((rows, HEAD_SIZE), jnp.float32),
        ],
        name="attend",
    )(query_rows, bias, *[array for array, _ in blocks])


def standard_body(ints_ref, gain_ref, down_ref, up_ref, noise_ref, *refs):
    pieces, own_ref, narrow_ref, masked_ref, log_ref = refs[:-4], *refs[-4:]
    rows, width = noise_ref.shape
    at = 0
    for ref in pieces:
        own_ref[:, at : at + ref.shape[1]] = ref[...]
        at += ref.shape[1]
    narrow = lax.dot_general(
        own_ref[...], down_ref[...], last_axis, preferred_element_type=jnp.float32
    ).astype(jnp.bfloat16)
    narrow_ref[...] = narrow
    position = ints_ref[0] + lax.broadcasted_iota(jnp.int32, (rows, 1), 0)
    keep = position < ints_ref[1]
    chunk = 512

    def step(c, total):
        start = pl.multiple_of(c * chunk, chunk)
        change = jnp.dot(
            narrow_ref[...], up_ref[:, pl.ds(start, chunk)], preferred_element_type=jnp.float32
        )
        noise = noise_ref[:, pl.ds(start, chunk)].astype(jnp.float32)
        standard = noise + gain_ref[0] * change
        masked_ref[:, pl.ds(start, chunk)] = jnp.where(keep, standard, 0.0).astype(jnp.bfloat16)
        terms = jnp.where(keep, noise * noise - standard * standard, 0.0)
        for col in range(0, chunk, 128):
            total = total + terms[:, col : col + 128]
        return total

    total = lax.fori_loop(0, width // chunk, step, jnp.zeros((rows, 128), jnp.float32))
    log_ref[...] = jnp.full(log_ref.shape, jnp.sum(total))


def products_body(ints_ref, narrow_ref, masked_ref, up_ref, own_ref, log_ref, *outs):
    width = masked_ref.shape[1]
    count = len(outs)
    columns = width // count
    own_columns = own_ref.shape[1] // count
    low_grad = lax.dot_general(
        masked_ref[...], up_ref[...], last_axis, preferred_element_type=jnp.float32
    ).astype(jnp.bfloat16)
    down = lax.dot_general(
        low_grad, own_ref[...], first_axis, preferred_element_type=jnp.float32
    )
    for k, out in enumerate(outs):
        start = pl.multiple_of(jnp.bitwise_xor(ints_ref[0], k) * columns, 128)
        out[:, :columns] = lax.dot_general(
            narrow_ref[...],
            masked_ref[:, pl.ds(start, columns)],
            first_axis,
            preferred_element_type=jnp.float32,
        )
        out[:, columns : columns + own_columns] = down[:, k * own_columns : (k + 1) * own_columns]
        out[:, columns + own_columns :] = jnp.broadcast_to(
            log_ref[:1], (out.shape[0], log_ref.shape[1])
        )


def rows_body(ints_ref, *refs):
    parts, up_ref, down_ref = refs[:-2], *refs[-2:]
    rows = parts[0].shape[0]
    columns = up_ref.shape[1]
    for k, ref in enumerate(parts):
        start = pl.multiple_of(jnp.bitwise_xor(ints_ref[0], k) * rows, 8)
        up_ref[pl.ds(start, rows)] = ref[:, :columns]
        down_ref[pl.ds(start, rows)] = ref[:, columns:]


def columns_body(ints_ref, *refs):
    parts, out_ref = refs[:-1], refs[-1]
    columns = parts[0].shape[1]
    for k, ref in enumerate(parts):
        start = pl.multiple_of(jnp.bitwise_xor(ints_ref[0], k) * columns, 128)
        out_ref[:, pl.ds(start, columns)] = ref[...]


def move_body(scalars_ref, own_ref, w_ref, latents_ref, noise_ref, out_ref):
    velocity = lax.dot_general(
        own_ref[...], w_ref[...], last_axis, preferred_element_type=jnp.float32
    )
    current = latents_ref[...].astype(jnp.float32)
    moved = current - scalars_ref[0] * (
        scalars_ref[1] * velocity + noise_level**2 * current / scalars_ref[2]
    )
    out_ref[...] = (moved + scalars_ref[3] * noise_ref[...].astype(jnp.float32)).astype(
        jnp.bfloat16
    )


def shards(
    latents,
    sampler_noise,
    query_key_value_weight,
    output_weight,
    adapter_down_map,
    adapter_up_map,
    valid_token_count,
    advantage,
    timestep_index,
):
    uly_count = lax.axis_size("uly")
    blk_count = lax.axis_size("blk")
    fsdp_count = lax.axis_size("fsdp")
    uly_id = lax.axis_index("uly")
    blk_id = lax.axis_index("blk")
    uly_int = jnp.reshape(uly_id, (1,)).astype(jnp.int32)
    blk_int = jnp.reshape(blk_id, (1,)).astype(jnp.int32)
    limit = valid_token_count[0]
    rank = adapter_down_map.shape[0]

    rows, width = latents.shape[1:]
    half = rows // 2
    video_slot = lax.axis_index("fsdp") % 4
    moved_a = gather_tokens(latents[0, :half])
    moved_b = gather_tokens(after(latents[0, half:], moved_a))
    work_limit = gather_tokens(jnp.full((8, 128), limit, jnp.int32))[0, 0]

    def norm(x):
        x = x.astype(jnp.float32)
        return (x * lax.rsqrt(jnp.mean(x * x, -1, keepdims=True) + rms_eps)).astype(jnp.bfloat16)

    normed_a, normed_b = norm(moved_a), norm(moved_b)
    heads_here = query_key_value_weight.shape[2] // HEAD_SIZE
    local_columns = heads_here * HEAD_SIZE
    pair = 2 * HEAD_SIZE
    group_rows = uly_count * rows

    weight = pl.pallas_call(
        arrange_body,
        out_shape=jax.ShapeDtypeStruct(
            (query_key_value_weight.shape[1], 3 * local_columns), jnp.bfloat16
        ),
        in_specs=[vmem],
        out_specs=vmem,
        name="arrange",
    )(query_key_value_weight)
    weight_rows = lax.all_gather(weight, "fsdp", axis=0, tiled=True)

    left_a = shift(normed_a, "uly", 1)
    right_a = shift(normed_a, "uly", -1)
    normed_b, relay, _ = lax.optimization_barrier((normed_b, left_a, right_a))
    up = shift(jnp.concatenate((relay, normed_b), 0), "uly", 1)
    right_b = shift(normed_b, "uly", -1)
    far_b = shift(right_b, "uly", -1)

    maps = after(jnp.concatenate((output_weight, adapter_down_map), 0), up, far_b)
    maps = jnp.concatenate([maps] + [exchange(maps, "uly", k) for k in (1, 2, 3)], 1)
    output_columns, down_full = maps[: output_weight.shape[0]], maps[output_weight.shape[0] :]

    key_values, query_rows = pl.pallas_call(
        project_body,
        out_shape=(
            jax.ShapeDtypeStruct((heads_here, group_rows, pair), jnp.bfloat16),
            jax.ShapeDtypeStruct((heads_here, group_rows, HEAD_SIZE), jnp.bfloat16),
        ),
        grid=(heads_here,),
        in_specs=[smem] + [vmem] * 7 + [pl.BlockSpec((width, local_columns), lambda h: (0, h))],
        out_specs=(
            pl.BlockSpec((None, group_rows, pair), lambda h: (h, 0, 0)),
            pl.BlockSpec((None, group_rows, HEAD_SIZE), lambda h: (h, 0, 0)),
        ),
        scratch_shapes=[pltpu.VMEM((group_rows, width), jnp.bfloat16)],
        name="project",
    )(uly_int, normed_a, normed_b, left_a, right_a, up, right_b, far_b, weight_rows)

    key_index = jnp.arange(blk_count * group_rows, dtype=jnp.int32)
    slot = video_slot ^ (key_index // group_rows)
    key_blk = jnp.zeros_like(slot)
    for p in range(blk_count):
        for q in range(4):
            key_blk = jnp.where((blk_id == p) & (slot == q), BLOCK[p][q], key_blk)
    key_pos = (
        (uly_id ^ (key_index % group_rows // rows)) * blk_count
        + key_blk
    ) * rows + key_index % rows
    bias = jnp.where(key_pos < work_limit, 0.0, -1e30).astype(jnp.float32)[None]

    lead = heads_here - 1
    core = exchange(key_values, "fsdp", 1)
    chip_lead = exchange(key_values[:lead], "fsdp", 2)
    chip_last = exchange(after(key_values[lead:], chip_lead), "fsdp", 2)
    far_lead = exchange(chip_lead, "fsdp", 1)
    far_last = exchange(chip_last, "fsdp", 1)
    weight_full = lax.all_gather(after(output_columns, chip_lead), "fsdp", axis=0, tiled=True)

    def others(segs):
        return [return_tokens(segs[k], k) for k in range(4)]

    segs = attend(
        query_rows, 0, lead, ((key_values, 0), (core, 0), (chip_lead, 0), (far_lead, 0)), bias
    )
    lead_pieces = others(segs)
    segs = attend(
        query_rows,
        lead,
        1,
        ((key_values, lead), (core, lead), (chip_last, 0), (far_last, 0)),
        bias,
    )
    last_pieces = others(segs)

    step_float = timestep_index[0].astype(jnp.float32)
    time_now = 1.0 - step_float / STEPS
    step_size = 1.0 / STEPS
    noise_std = noise_level * jnp.sqrt(time_now / (1.0 - time_now))
    drift_gain = 1.0 + noise_level**2 / 2.0
    ratio_gain = jnp.sqrt(step_size) * drift_gain / noise_std
    valid_len = limit.astype(jnp.float32)
    ints = jnp.stack([(uly_id * blk_count + blk_id) * rows, limit]).astype(jnp.int32)
    pieces = [p for both in zip(lead_pieces, last_pieces) for p in both]
    own_heads, narrow_projection, masked, log_tile = pl.pallas_call(
        standard_body,
        out_shape=(
            jax.ShapeDtypeStruct((rows, uly_count * local_columns), jnp.bfloat16),
            jax.ShapeDtypeStruct((rows, rank), jnp.bfloat16),
            jax.ShapeDtypeStruct((rows, width), jnp.bfloat16),
            jax.ShapeDtypeStruct((8, 128), jnp.float32),
        ),
        in_specs=[smem, smem] + [vmem] * (3 + len(pieces)),
        out_specs=(vmem,) * 4,
        name="standard",
    )(ints, jnp.reshape(ratio_gain, (1,)), down_full, adapter_up_map, sampler_noise[0], *pieces)

    up_columns = width // uly_count
    share_columns = up_columns + local_columns
    shares = pl.pallas_call(
        products_body,
        out_shape=[jax.ShapeDtypeStruct((rank, share_columns + 128), jnp.float32)] * uly_count,
        in_specs=[smem] + [vmem] * 5,
        out_specs=[vmem] * uly_count,
        name="products",
    )(uly_int, narrow_projection, masked, adapter_up_map, own_heads, log_tile)

    parts = [exchange(shares[k], "uly", k) for k in (1, 2, 3)]
    tile = 512
    scalars = jnp.stack(
        [
            jnp.float32(step_size),
            jnp.float32(drift_gain),
            2.0 * (1.0 - time_now),
            noise_std * jnp.sqrt(step_size),
        ]
    )
    token_tile = pl.BlockSpec((rows, tile), lambda i: (0, i))
    next_latents = pl.pallas_call(
        move_body,
        out_shape=jax.ShapeDtypeStruct((rows, width), jnp.bfloat16),
        grid=(width // tile,),
        in_specs=[
            smem,
            pl.BlockSpec(own_heads.shape, lambda i: (0, 0)),
            pl.BlockSpec((tile, own_heads.shape[1]), lambda i: (i, 0)),
            token_tile,
            token_tile,
        ],
        out_specs=token_tile,
        name="move",
    )(scalars, own_heads, weight_full, latents[0], sampler_noise[0])
    next_latents, *parts = lax.optimization_barrier((next_latents, *parts))
    summed = four_sum([shares[0]] + parts)
    part = rank // blk_count

    def rows_of(k):
        return lax.dynamic_slice_in_dim(summed, (blk_id ^ k) * part, part, 0)

    summed = four_sum([rows_of(0)] + [exchange(rows_of(k), "blk", k) for k in (1, 2, 3)])
    log_ratio = summed[0, share_columns] / (2.0 * valid_len * width)
    coef = (
        loss_scale
        * advantage[0]
        * jnp.exp(log_ratio)
        * ratio_gain
        / (fsdp_count * valid_len * width)
    )
    summed = summed[:, :share_columns] * coef
    for unit in (4, 1):
        summed = four_sum([summed] + [exchange(summed, "fsdp", unit * k) for k in (1, 2, 3)])

    parts = [exchange(summed, "blk", k) for k in (1, 2, 3)]
    up_mine, grad_down = pl.pallas_call(
        rows_body,
        out_shape=(
            jax.ShapeDtypeStruct((rank, up_columns), jnp.float32),
            jax.ShapeDtypeStruct((rank, local_columns), jnp.float32),
        ),
        in_specs=[smem] + [vmem] * 4,
        out_specs=(vmem,) * 2,
        name="rows",
    )(blk_int, summed, *parts)
    grad_up = pl.pallas_call(
        columns_body,
        out_shape=jax.ShapeDtypeStruct((rank, width), jnp.float32),
        in_specs=[smem] + [vmem] * 4,
        out_specs=vmem,
        name="columns",
    )(uly_int, up_mine, *[exchange(up_mine, "uly", k) for k in (1, 2, 3)])
    return (next_latents[None], jnp.reshape(log_ratio, (1,)), grad_down, grad_up)


def solution(mesh):
    placed = (
        P("fsdp", ("uly", "blk"), None),
        P("fsdp", ("uly", "blk"), None),
        P(None, "fsdp", "uly"),
        P("fsdp", "uly"),
        P(None, "uly"),
        P(),
        P("fsdp"),
        P("fsdp"),
        P(),
    )

    return jax.shard_map(
        shards,
        mesh=mesh,
        in_specs=placed,
        out_specs=(P("fsdp", ("uly", "blk"), None), P("fsdp"), P(None, "uly"), P()),
        check_vma=False,
    )
```

```python
import math

import jax
import jax.numpy as jnp
from jax import lax
from jax.experimental import pallas as pl
from jax.experimental.pallas import tpu as pltpu
from jax.sharding import PartitionSpec as P


HEAD_SIZE = 128
STEPS = 16

noise_level = 0.7
loss_scale = 4194304.0
rms_eps = 1e-06


smem = pl.BlockSpec(memory_space=pltpu.SMEM)
vmem = pl.BlockSpec(memory_space=pltpu.VMEM)
last_axis = (((1,), (1,)), ((), ()))
first_axis = (((0,), (0,)), ((), ()))


PLACE = (0, 2, 1, 3)
SLOT = ((0, 2, 3, 1), (2, 0, 1, 3), (0, 2, 3, 1), (2, 0, 1, 3))
VIDEO = [PLACE.index(p) for p in range(4)]
BLOCK = [[SLOT[VIDEO[p]].index(q) for q in range(4)] for p in range(4)]


def worker(f, b):
    w = f % 4
    return f - w + SLOT[w][b], PLACE[w]


def gather_tokens(x):
    count = lax.axis_size("blk")
    pairs = []
    for f in range(lax.axis_size("fsdp")):
        for b in range(count):
            to_f, to_b = worker(f, b)
            pairs.append((f * count + b, to_f * count + to_b))
    return lax.ppermute(x, ("fsdp", "blk"), pairs)


def return_tokens(x, mask):
    blks, ulys = lax.axis_size("blk"), lax.axis_size("uly")
    pairs = []
    for f in range(lax.axis_size("fsdp")):
        for b in range(blks):
            to_f, to_b = worker(f, b)
            for u in range(ulys):
                pairs.append(
                    ((to_f * ulys + u) * blks + to_b, (f * ulys + (u ^ mask)) * blks + b)
                )
    return lax.ppermute(x, ("fsdp", "uly", "blk"), pairs)


def shift(x, axis, step):
    n = lax.axis_size(axis)
    return lax.ppermute(x, axis, [(i, (i + step) % n) for i in range(n)])


def exchange(x, axis, mask):
    n = lax.axis_size(axis)
    return lax.ppermute(x, axis, [(i, i ^ mask) for i in range(n)])


def after(x, *earlier):
    return lax.optimization_barrier((x,) + earlier)[0]


def four_sum(parts):
    return (parts[0] + parts[1]) + (parts[2] + parts[3])


def arrange_body(w_ref, out_ref):
    at = 0
    for start in range(0, w_ref.shape[2], HEAD_SIZE):
        for j in range(3):
            out_ref[:, at : at + HEAD_SIZE] = w_ref[j, :, start : start + HEAD_SIZE]
            at += HEAD_SIZE


def project_body(
    ints_ref, a_ref, b_ref, left_a_ref, right_a_ref, up_ref, right_b_ref, far_b_ref, w_ref,
    pairs_ref, query_ref, all_ref,
):
    half = a_ref.shape[0]
    rows = 2 * half

    @pl.when(pl.program_id(0) == 0)
    def _():
        odd = lax.rem(ints_ref[0], 2)
        left = pl.multiple_of((3 - 2 * odd) * rows, half)
        right = pl.multiple_of((1 + 2 * odd) * rows, half)
        all_ref[:half] = a_ref[...]
        all_ref[half:rows] = b_ref[...]
        all_ref[pl.ds(left, half)] = left_a_ref[...]
        all_ref[pl.ds(left + half, half)] = up_ref[half:]
        all_ref[pl.ds(right, half)] = right_a_ref[...]
        all_ref[pl.ds(right + half, half)] = right_b_ref[...]
        all_ref[2 * rows : 2 * rows + half] = up_ref[:half]
        all_ref[2 * rows + half : 3 * rows] = far_b_ref[...]

    tile = 384

    def step(r, carry):
        start = pl.multiple_of(r * tile, tile)
        out = jnp.dot(
            all_ref[pl.ds(start, tile)], w_ref[...], preferred_element_type=jnp.float32
        ).astype(jnp.bfloat16)
        query_ref[pl.ds(start, tile)] = out[:, :HEAD_SIZE]
        pairs_ref[pl.ds(start, tile)] = out[:, HEAD_SIZE:]
        return carry

    lax.fori_loop(0, all_ref.shape[0] // tile, step, 0)


def attention_body(q_ref, bias_ref, *refs):
    blocks, earlier = refs[:4], refs[4:-7]
    outs, (pairs_ref, scores_ref, acc_ref) = refs[-7:-3], refs[-3:]
    scale = math.log2(math.e) / math.sqrt(HEAD_SIZE)
    at = 0
    for ref in blocks:
        pairs_ref[at : at + ref.shape[0]] = ref[...]
        at += ref.shape[0]
    chunk = scores_ref.shape[2]
    count = scores_ref.shape[0]
    rows = q_ref.shape[0]

    def score(c, top):
        start = pl.multiple_of(c * chunk, chunk)
        s = lax.dot_general(
            q_ref[...],
            pairs_ref[pl.ds(start, chunk), :HEAD_SIZE],
            last_axis,
            preferred_element_type=jnp.float32,
        )
        s = s + bias_ref[:, pl.ds(start, chunk)]
        scores_ref[c] = s
        for col in range(0, chunk, 128):
            top = jnp.maximum(top, s[:, col : col + 128])
        return top

    top = lax.fori_loop(0, count, score, jnp.full((rows, 128), -jnp.inf, jnp.float32))
    top = jnp.max(top, -1, keepdims=True) * scale
    acc_ref[...] = jnp.zeros_like(acc_ref)

    def collect(c, total):
        start = pl.multiple_of(c * chunk, chunk)
        p = jnp.exp2(scores_ref[c] * scale - top)
        for col in range(0, chunk, 128):
            total = total + p[:, col : col + 128]
        acc_ref[...] += jnp.dot(
            p.astype(jnp.bfloat16),
            pairs_ref[pl.ds(start, chunk), HEAD_SIZE:],
            preferred_element_type=jnp.float32,
        )
        return total

    total = lax.fori_loop(0, count, collect, jnp.zeros((rows, 128), jnp.float32))
    out = (acc_ref[...] / jnp.sum(total, -1, keepdims=True)).astype(jnp.bfloat16)
    seg = rows // len(outs)
    for k, ref in enumerate(outs):
        ref[:, -HEAD_SIZE:] = out[k * seg : (k + 1) * seg]
    for ref, before in zip(outs, earlier):
        ref[:, :-HEAD_SIZE] = before[...]


def attend(query_rows, first_head, heads, blocks, bias, earlier=()):
    rows = query_rows.shape[1]
    keys = bias.shape[1]
    seg = rows // 4
    columns = heads * HEAD_SIZE + sum(array.shape[1] for array in earlier[:1])
    chunk = 1024

    def spec(array, place):
        return pl.BlockSpec((None,) + array.shape[1:], lambda i: (i + place, 0, 0))

    return pl.pallas_call(
        attention_body,
        out_shape=[jax.ShapeDtypeStruct((seg, columns), jnp.bfloat16)] * 4,
        grid=(heads,),
        in_specs=[
            pl.BlockSpec((None, rows, HEAD_SIZE), lambda i: (i + first_head, 0, 0)),
            pl.BlockSpec(bias.shape, lambda i: (0, 0)),
        ]
        + [spec(array, place) for array, place in blocks]
        + [pl.BlockSpec(array.shape, lambda i: (0, 0)) for array in earlier],
        out_specs=[pl.BlockSpec((seg, columns // heads), lambda i: (0, i))] * 4,
        scratch_shapes=[
            pltpu.VMEM((keys, 2 * HEAD_SIZE), jnp.bfloat16),
            pltpu.VMEM((keys // chunk, rows, chunk), jnp.float32),
            pltpu.VMEM((rows, HEAD_SIZE), jnp.float32),
        ],
        name="attend",
    )(query_rows, bias, *[array for array, _ in blocks], *earlier)


def standard_body(ints_ref, gain_ref, down_ref, up_ref, noise_ref, *refs):
    pieces, own_ref, narrow_ref, masked_ref, log_ref = refs[:-4], *refs[-4:]
    rows, width = noise_ref.shape
    at = 0
    for ref in pieces:
        own_ref[:, at : at + ref.shape[1]] = ref[...]
        at += ref.shape[1]
    narrow = lax.dot_general(
        own_ref[...], down_ref[...], last_axis, preferred_element_type=jnp.float32
    ).astype(jnp.bfloat16)
    narrow_ref[...] = narrow
    position = ints_ref[0] + lax.broadcasted_iota(jnp.int32, (rows, 1), 0)
    keep = position < ints_ref[1]
    chunk = 512

    def step(c, total):
        start = pl.multiple_of(c * chunk, chunk)
        change = jnp.dot(
            narrow_ref[...], up_ref[:, pl.ds(start, chunk)], preferred_element_type=jnp.float32
        )
        noise = noise_ref[:, pl.ds(start, chunk)].astype(jnp.float32)
        standard = noise + gain_ref[0] * change
        masked_ref[:, pl.ds(start, chunk)] = jnp.where(keep, standard, 0.0).astype(jnp.bfloat16)
        terms = jnp.where(keep, noise * noise - standard * standard, 0.0)
        for col in range(0, chunk, 128):
            total = total + terms[:, col : col + 128]
        return total

    total = lax.fori_loop(0, width // chunk, step, jnp.zeros((rows, 128), jnp.float32))
    log_ref[...] = jnp.full(log_ref.shape, jnp.sum(total))


def products_body(ints_ref, narrow_ref, masked_ref, up_ref, own_ref, log_ref, *outs):
    width = masked_ref.shape[1]
    count = len(outs)
    columns = width // count
    own_columns = own_ref.shape[1] // count
    low_grad = lax.dot_general(
        masked_ref[...], up_ref[...], last_axis, preferred_element_type=jnp.float32
    ).astype(jnp.bfloat16)
    down = lax.dot_general(
        low_grad, own_ref[...], first_axis, preferred_element_type=jnp.float32
    )
    for k, out in enumerate(outs):
        start = pl.multiple_of(jnp.bitwise_xor(ints_ref[0], k) * columns, 128)
        out[:, :columns] = lax.dot_general(
            narrow_ref[...],
            masked_ref[:, pl.ds(start, columns)],
            first_axis,
            preferred_element_type=jnp.float32,
        )
        out[:, columns : columns + own_columns] = down[:, k * own_columns : (k + 1) * own_columns]
        out[:, columns + own_columns :] = jnp.broadcast_to(
            log_ref[:1], (out.shape[0], log_ref.shape[1])
        )


def rows_body(ints_ref, *refs):
    parts, up_ref, down_ref = refs[:-2], *refs[-2:]
    rows = parts[0].shape[0]
    columns = up_ref.shape[1]
    for k, ref in enumerate(parts):
        start = pl.multiple_of(jnp.bitwise_xor(ints_ref[0], k) * rows, 16)
        up_ref[pl.ds(start, rows)] = ref[:, :columns]
        down_ref[pl.ds(start, rows)] = ref[:, columns:].astype(jnp.float32)


def columns_body(ints_ref, *refs):
    parts, out_ref = refs[:-1], refs[-1]
    columns = parts[0].shape[1]
    for k, ref in enumerate(parts):
        start = pl.multiple_of(jnp.bitwise_xor(ints_ref[0], k) * columns, 128)
        out_ref[:, pl.ds(start, columns)] = ref[...].astype(jnp.float32)


def move_body(scalars_ref, own_ref, w_ref, latents_ref, noise_ref, out_ref):
    velocity = lax.dot_general(
        own_ref[...], w_ref[...], last_axis, preferred_element_type=jnp.float32
    )
    current = latents_ref[...].astype(jnp.float32)
    moved = current - scalars_ref[0] * (
        scalars_ref[1] * velocity + noise_level**2 * current / scalars_ref[2]
    )
    out_ref[...] = (moved + scalars_ref[3] * noise_ref[...].astype(jnp.float32)).astype(
        jnp.bfloat16
    )


def shards(
    latents,
    sampler_noise,
    query_key_value_weight,
    output_weight,
    adapter_down_map,
    adapter_up_map,
    valid_token_count,
    advantage,
    timestep_index,
):
    uly_count = lax.axis_size("uly")
    blk_count = lax.axis_size("blk")
    fsdp_count = lax.axis_size("fsdp")
    uly_id = lax.axis_index("uly")
    blk_id = lax.axis_index("blk")
    uly_int = jnp.reshape(uly_id, (1,)).astype(jnp.int32)
    blk_int = jnp.reshape(blk_id, (1,)).astype(jnp.int32)
    limit = valid_token_count[0]
    rank = adapter_down_map.shape[0]

    rows, width = latents.shape[1:]
    half = rows // 2
    video_slot = lax.axis_index("fsdp") % 4
    moved_a = gather_tokens(latents[0, :half])
    moved_b = gather_tokens(after(latents[0, half:], moved_a))
    work_limit = gather_tokens(jnp.full((8, 128), limit, jnp.int32))[0, 0]

    def norm(x):
        x = x.astype(jnp.float32)
        return (x * lax.rsqrt(jnp.mean(x * x, -1, keepdims=True) + rms_eps)).astype(jnp.bfloat16)

    normed_a, normed_b = norm(moved_a), norm(moved_b)
    heads_here = query_key_value_weight.shape[2] // HEAD_SIZE
    local_columns = heads_here * HEAD_SIZE
    pair = 2 * HEAD_SIZE
    group_rows = uly_count * rows

    weight = pl.pallas_call(
        arrange_body,
        out_shape=jax.ShapeDtypeStruct(
            (query_key_value_weight.shape[1], 3 * local_columns), jnp.bfloat16
        ),
        in_specs=[vmem],
        out_specs=vmem,
        name="arrange",
    )(query_key_value_weight)
    weight_rows = lax.all_gather(weight, "fsdp", axis=0, tiled=True)

    left_a = shift(normed_a, "uly", 1)
    right_a = shift(normed_a, "uly", -1)
    normed_b, relay, _ = lax.optimization_barrier((normed_b, left_a, right_a))
    up = shift(jnp.concatenate((relay, normed_b), 0), "uly", 1)
    right_b = shift(normed_b, "uly", -1)
    far_b = shift(right_b, "uly", -1)

    maps = after(jnp.concatenate((output_weight, adapter_down_map), 0), up, far_b)
    maps = jnp.concatenate([maps] + [exchange(maps, "uly", k) for k in (1, 2, 3)], 1)
    output_columns, down_full = maps[: output_weight.shape[0]], maps[output_weight.shape[0] :]

    key_values, query_rows = pl.pallas_call(
        project_body,
        out_shape=(
            jax.ShapeDtypeStruct((heads_here, group_rows, pair), jnp.bfloat16),
            jax.ShapeDtypeStruct((heads_here, group_rows, HEAD_SIZE), jnp.bfloat16),
        ),
        grid=(heads_here,),
        in_specs=[smem] + [vmem] * 7 + [pl.BlockSpec((width, local_columns), lambda h: (0, h))],
        out_specs=(
            pl.BlockSpec((None, group_rows, pair), lambda h: (h, 0, 0)),
            pl.BlockSpec((None, group_rows, HEAD_SIZE), lambda h: (h, 0, 0)),
        ),
        scratch_shapes=[pltpu.VMEM((group_rows, width), jnp.bfloat16)],
        name="project",
    )(uly_int, normed_a, normed_b, left_a, right_a, up, right_b, far_b, weight_rows)

    key_index = jnp.arange(blk_count * group_rows, dtype=jnp.int32)
    slot = video_slot ^ (key_index // group_rows)
    key_blk = jnp.zeros_like(slot)
    for p in range(blk_count):
        for q in range(4):
            key_blk = jnp.where((blk_id == p) & (slot == q), BLOCK[p][q], key_blk)
    key_pos = (
        (uly_id ^ (key_index % group_rows // rows)) * blk_count
        + key_blk
    ) * rows + key_index % rows
    bias = jnp.where(key_pos < work_limit, 0.0, -1e30).astype(jnp.float32)[None]

    lead = heads_here - 1
    core = exchange(key_values, "fsdp", 1)
    chip_lead = exchange(key_values[:lead], "fsdp", 2)
    chip_last = exchange(after(key_values[lead:], chip_lead), "fsdp", 2)
    far_lead = exchange(chip_lead, "fsdp", 1)
    far_last = exchange(chip_last, "fsdp", 1)
    weight_full = lax.all_gather(after(output_columns, chip_lead), "fsdp", axis=0, tiled=True)

    segs = attend(
        query_rows, 0, lead, ((key_values, 0), (core, 0), (chip_lead, 0), (far_lead, 0)), bias
    )
    segs = attend(
        query_rows,
        lead,
        1,
        ((key_values, lead), (core, lead), (chip_last, 0), (far_last, 0)),
        bias,
        segs,
    )
    pieces = [return_tokens(segs[k], k) for k in range(uly_count)]

    step_float = timestep_index[0].astype(jnp.float32)
    time_now = 1.0 - step_float / STEPS
    step_size = 1.0 / STEPS
    noise_std = noise_level * jnp.sqrt(time_now / (1.0 - time_now))
    drift_gain = 1.0 + noise_level**2 / 2.0
    ratio_gain = jnp.sqrt(step_size) * drift_gain / noise_std
    valid_len = limit.astype(jnp.float32)
    ints = jnp.stack([(uly_id * blk_count + blk_id) * rows, limit]).astype(jnp.int32)
    own_heads, narrow_projection, masked, log_tile = pl.pallas_call(
        standard_body,
        out_shape=(
            jax.ShapeDtypeStruct((rows, uly_count * local_columns), jnp.bfloat16),
            jax.ShapeDtypeStruct((rows, rank), jnp.bfloat16),
            jax.ShapeDtypeStruct((rows, width), jnp.bfloat16),
            jax.ShapeDtypeStruct((8, 128), jnp.float32),
        ),
        in_specs=[smem, smem] + [vmem] * (3 + len(pieces)),
        out_specs=(vmem,) * 4,
        name="standard",
    )(ints, jnp.reshape(ratio_gain, (1,)), down_full, adapter_up_map, sampler_noise[0], *pieces)

    up_columns = width // uly_count
    share_columns = up_columns + local_columns
    shares = pl.pallas_call(
        products_body,
        out_shape=[jax.ShapeDtypeStruct((rank, share_columns + 128), jnp.float32)] * uly_count,
        in_specs=[smem] + [vmem] * 5,
        out_specs=[vmem] * uly_count,
        name="products",
    )(uly_int, narrow_projection, masked, adapter_up_map, own_heads, log_tile)

    parts = [exchange(shares[k], "uly", k) for k in (1, 2, 3)]
    tile = 512
    scalars = jnp.stack(
        [
            jnp.float32(step_size),
            jnp.float32(drift_gain),
            2.0 * (1.0 - time_now),
            noise_std * jnp.sqrt(step_size),
        ]
    )
    token_tile = pl.BlockSpec((rows, tile), lambda i: (0, i))
    next_latents = pl.pallas_call(
        move_body,
        out_shape=jax.ShapeDtypeStruct((rows, width), jnp.bfloat16),
        grid=(width // tile,),
        in_specs=[
            smem,
            pl.BlockSpec(own_heads.shape, lambda i: (0, 0)),
            pl.BlockSpec((tile, own_heads.shape[1]), lambda i: (i, 0)),
            token_tile,
            token_tile,
        ],
        out_specs=token_tile,
        name="move",
    )(scalars, own_heads, weight_full, latents[0], sampler_noise[0])
    next_latents, *parts = lax.optimization_barrier((next_latents, *parts))
    summed = four_sum([shares[0]] + parts)
    part = rank // blk_count

    def rows_of(k):
        return lax.dynamic_slice_in_dim(summed, (blk_id ^ k) * part, part, 0)

    summed = four_sum([rows_of(0)] + [exchange(rows_of(k), "blk", k) for k in (1, 2, 3)])
    log_ratio = summed[0, share_columns] / (2.0 * valid_len * width)
    coef = (
        loss_scale
        * advantage[0]
        * jnp.exp(log_ratio)
        * ratio_gain
        / (fsdp_count * valid_len * width)
    )
    summed = summed[:, :share_columns] * coef
    for unit in (4, 1):
        summed = four_sum([summed] + [exchange(summed, "fsdp", unit * k) for k in (1, 2, 3)])

    summed = summed.astype(jnp.bfloat16)
    parts = [exchange(summed, "blk", k) for k in (1, 2, 3)]
    up_mine, grad_down = pl.pallas_call(
        rows_body,
        out_shape=(
            jax.ShapeDtypeStruct((rank, up_columns), jnp.bfloat16),
            jax.ShapeDtypeStruct((rank, local_columns), jnp.float32),
        ),
        in_specs=[smem] + [vmem] * 4,
        out_specs=(vmem,) * 2,
        name="rows",
    )(blk_int, summed, *parts)
    grad_up = pl.pallas_call(
        columns_body,
        out_shape=jax.ShapeDtypeStruct((rank, width), jnp.float32),
        in_specs=[smem] + [vmem] * 4,
        out_specs=vmem,
        name="columns",
    )(uly_int, up_mine, *[exchange(up_mine, "uly", k) for k in (1, 2, 3)])
    return (next_latents[None], jnp.reshape(log_ratio, (1,)), grad_down, grad_up)


def solution(mesh):
    placed = (
        P("fsdp", ("uly", "blk"), None),
        P("fsdp", ("uly", "blk"), None),
        P(None, "fsdp", "uly"),
        P("fsdp", "uly"),
        P(None, "uly"),
        P(),
        P("fsdp"),
        P("fsdp"),
        P(),
    )

    return jax.shard_map(
        shards,
        mesh=mesh,
        in_specs=placed,
        out_specs=(P("fsdp", ("uly", "blk"), None), P("fsdp"), P(None, "uly"), P()),
        check_vma=False,
    )
```

```python
import math

import jax
import jax.numpy as jnp
from jax import lax
from jax.experimental import pallas as pl
from jax.experimental.pallas import tpu as pltpu
from jax.sharding import PartitionSpec as P


HEAD_SIZE = 128
STEPS = 16

noise_level = 0.7
loss_scale = 4194304.0
rms_eps = 1e-06


smem = pl.BlockSpec(memory_space=pltpu.SMEM)
vmem = pl.BlockSpec(memory_space=pltpu.VMEM)
last_axis = (((1,), (1,)), ((), ()))
first_axis = (((0,), (0,)), ((), ()))


PLACE = (0, 2, 1, 3)
SLOT = ((0, 2, 3, 1), (2, 0, 1, 3), (0, 2, 3, 1), (2, 0, 1, 3))
VIDEO = [PLACE.index(p) for p in range(4)]
BLOCK = [[SLOT[VIDEO[p]].index(q) for q in range(4)] for p in range(4)]


def worker(f, b):
    w = f % 4
    return f - w + SLOT[w][b], PLACE[w]


def gather_tokens(x):
    count = lax.axis_size("blk")
    pairs = []
    for f in range(lax.axis_size("fsdp")):
        for b in range(count):
            to_f, to_b = worker(f, b)
            pairs.append((f * count + b, to_f * count + to_b))
    return lax.ppermute(x, ("fsdp", "blk"), pairs)


def return_tokens(x, mask):
    blks, ulys = lax.axis_size("blk"), lax.axis_size("uly")
    pairs = []
    for f in range(lax.axis_size("fsdp")):
        for b in range(blks):
            to_f, to_b = worker(f, b)
            for u in range(ulys):
                pairs.append(
                    ((to_f * ulys + u) * blks + to_b, (f * ulys + (u ^ mask)) * blks + b)
                )
    return lax.ppermute(x, ("fsdp", "uly", "blk"), pairs)


def shift(x, axis, step):
    n = lax.axis_size(axis)
    return lax.ppermute(x, axis, [(i, (i + step) % n) for i in range(n)])


def exchange(x, axis, mask):
    n = lax.axis_size(axis)
    return lax.ppermute(x, axis, [(i, i ^ mask) for i in range(n)])


def after(x, *earlier):
    return lax.optimization_barrier((x,) + earlier)[0]


def four_sum(parts):
    return (parts[0] + parts[1]) + (parts[2] + parts[3])


def arrange_body(w_ref, out_ref):
    at = 0
    for start in range(0, w_ref.shape[2], HEAD_SIZE):
        for j in range(3):
            out_ref[:, at : at + HEAD_SIZE] = w_ref[j, :, start : start + HEAD_SIZE]
            at += HEAD_SIZE


def project_body(
    ints_ref, a_ref, b_ref, left_a_ref, right_a_ref, up_ref, right_b_ref, far_b_ref, w_ref,
    pairs_ref, query_ref, all_ref,
):
    half = a_ref.shape[0]
    rows = 2 * half

    @pl.when(pl.program_id(0) == 0)
    def _():
        odd = lax.rem(ints_ref[0], 2)
        left = pl.multiple_of((3 - 2 * odd) * rows, half)
        right = pl.multiple_of((1 + 2 * odd) * rows, half)
        all_ref[:half] = a_ref[...]
        all_ref[half:rows] = b_ref[...]
        all_ref[pl.ds(left, half)] = left_a_ref[...]
        all_ref[pl.ds(left + half, half)] = up_ref[half:]
        all_ref[pl.ds(right, half)] = right_a_ref[...]
        all_ref[pl.ds(right + half, half)] = right_b_ref[...]
        all_ref[2 * rows : 2 * rows + half] = up_ref[:half]
        all_ref[2 * rows + half : 3 * rows] = far_b_ref[...]

    tile = 384

    def step(r, carry):
        start = pl.multiple_of(r * tile, tile)
        out = jnp.dot(
            all_ref[pl.ds(start, tile)], w_ref[...], preferred_element_type=jnp.float32
        ).astype(jnp.bfloat16)
        query_ref[pl.ds(start, tile)] = out[:, :HEAD_SIZE]
        pairs_ref[pl.ds(start, tile)] = out[:, HEAD_SIZE:]
        return carry

    lax.fori_loop(0, all_ref.shape[0] // tile, step, 0)


def attention_body(q_ref, bias_ref, *refs):
    blocks, earlier = refs[:4], refs[4:-7]
    outs, (pairs_ref, scores_ref, acc_ref) = refs[-7:-3], refs[-3:]
    scale = math.log2(math.e) / math.sqrt(HEAD_SIZE)
    at = 0
    for ref in blocks:
        pairs_ref[at : at + ref.shape[0]] = ref[...]
        at += ref.shape[0]
    chunk = scores_ref.shape[2]
    count = scores_ref.shape[0]
    rows = q_ref.shape[0]

    def score(c, top):
        start = pl.multiple_of(c * chunk, chunk)
        s = lax.dot_general(
            q_ref[...],
            pairs_ref[pl.ds(start, chunk), :HEAD_SIZE],
            last_axis,
            preferred_element_type=jnp.float32,
        )
        s = s + bias_ref[:, pl.ds(start, chunk)]
        scores_ref[c] = s
        for col in range(0, chunk, 128):
            top = jnp.maximum(top, s[:, col : col + 128])
        return top

    top = lax.fori_loop(0, count, score, jnp.full((rows, 128), -jnp.inf, jnp.float32))
    top = jnp.max(top, -1, keepdims=True) * scale
    acc_ref[...] = jnp.zeros_like(acc_ref)

    def collect(c, total):
        start = pl.multiple_of(c * chunk, chunk)
        p = jnp.exp2(scores_ref[c] * scale - top)
        for col in range(0, chunk, 128):
            total = total + p[:, col : col + 128]
        acc_ref[...] += jnp.dot(
            p.astype(jnp.bfloat16),
            pairs_ref[pl.ds(start, chunk), HEAD_SIZE:],
            preferred_element_type=jnp.float32,
        )
        return total

    total = lax.fori_loop(0, count, collect, jnp.zeros((rows, 128), jnp.float32))
    out = (acc_ref[...] / jnp.sum(total, -1, keepdims=True)).astype(jnp.bfloat16)
    seg = rows // len(outs)
    for k, ref in enumerate(outs):
        ref[:, -HEAD_SIZE:] = out[k * seg : (k + 1) * seg]
    for ref, before in zip(outs, earlier):
        ref[:, :-HEAD_SIZE] = before[...]


def attend(queries, blocks, bias, earlier=()):
    heads, rows, _ = queries.shape
    keys = bias.shape[1]
    seg = rows // 4
    columns = heads * HEAD_SIZE + sum(array.shape[1] for array in earlier[:1])
    chunk = 1024

    def spec(array):
        return pl.BlockSpec((None,) + array.shape[1:], lambda i: (i, 0, 0))

    return pl.pallas_call(
        attention_body,
        out_shape=[jax.ShapeDtypeStruct((seg, columns), jnp.bfloat16)] * 4,
        grid=(heads,),
        in_specs=[spec(queries), pl.BlockSpec(bias.shape, lambda i: (0, 0))]
        + [spec(array) for array in blocks]
        + [pl.BlockSpec(array.shape, lambda i: (0, 0)) for array in earlier],
        out_specs=[pl.BlockSpec((seg, columns // heads), lambda i: (0, i))] * 4,
        scratch_shapes=[
            pltpu.VMEM((keys, 2 * HEAD_SIZE), jnp.bfloat16),
            pltpu.VMEM((keys // chunk, rows, chunk), jnp.float32),
            pltpu.VMEM((rows, HEAD_SIZE), jnp.float32),
        ],
        name="attend",
    )(queries, bias, *blocks, *earlier)


def standard_body(ints_ref, gain_ref, down_ref, up_ref, noise_ref, *refs):
    pieces, own_ref, narrow_ref, masked_ref, log_ref = refs[:-4], *refs[-4:]
    rows, width = noise_ref.shape
    at = 0
    for ref in pieces:
        own_ref[:, at : at + ref.shape[1]] = ref[...]
        at += ref.shape[1]
    narrow = lax.dot_general(
        own_ref[...], down_ref[...], last_axis, preferred_element_type=jnp.float32
    ).astype(jnp.bfloat16)
    narrow_ref[...] = narrow
    position = ints_ref[0] + lax.broadcasted_iota(jnp.int32, (rows, 1), 0)
    keep = position < ints_ref[1]
    chunk = 512

    def step(c, total):
        start = pl.multiple_of(c * chunk, chunk)
        change = jnp.dot(
            narrow_ref[...], up_ref[:, pl.ds(start, chunk)], preferred_element_type=jnp.float32
        )
        noise = noise_ref[:, pl.ds(start, chunk)].astype(jnp.float32)
        standard = noise + gain_ref[0] * change
        masked_ref[:, pl.ds(start, chunk)] = jnp.where(keep, standard, 0.0).astype(jnp.bfloat16)
        terms = jnp.where(keep, noise * noise - standard * standard, 0.0)
        for col in range(0, chunk, 128):
            total = total + terms[:, col : col + 128]
        return total

    total = lax.fori_loop(0, width // chunk, step, jnp.zeros((rows, 128), jnp.float32))
    log_ref[...] = jnp.full(log_ref.shape, jnp.sum(total))


def products_body(ints_ref, narrow_ref, masked_ref, up_ref, own_ref, log_ref, *outs):
    log = jnp.broadcast_to(log_ref[:1], (outs[0].shape[0], log_ref.shape[1]))
    column = lax.broadcasted_iota(jnp.int32, log.shape, 1)
    high = log.astype(jnp.bfloat16)
    rest = log - high.astype(jnp.float32)
    middle = rest.astype(jnp.bfloat16)
    low = (rest - middle.astype(jnp.float32)).astype(jnp.bfloat16)
    terms = jnp.where(column == 0, high, jnp.where(column == 1, middle, low))
    width = masked_ref.shape[1]
    count = len(outs)
    columns = width // count
    own_columns = own_ref.shape[1] // count
    low_grad = lax.dot_general(
        masked_ref[...], up_ref[...], last_axis, preferred_element_type=jnp.float32
    ).astype(jnp.bfloat16)
    down = lax.dot_general(
        low_grad, own_ref[...], first_axis, preferred_element_type=jnp.float32
    )
    for k, out in enumerate(outs):
        start = pl.multiple_of(jnp.bitwise_xor(ints_ref[0], k) * columns, 128)
        out[:, :columns] = lax.dot_general(
            narrow_ref[...],
            masked_ref[:, pl.ds(start, columns)],
            first_axis,
            preferred_element_type=jnp.float32,
        ).astype(jnp.bfloat16)
        out[:, columns : columns + own_columns] = down[
            :, k * own_columns : (k + 1) * own_columns
        ].astype(jnp.bfloat16)
        out[:, columns + own_columns :] = terms


def rows_body(ints_ref, *refs):
    parts, up_ref, down_ref = refs[:-2], *refs[-2:]
    rows = parts[0].shape[0]
    columns = up_ref.shape[1]
    for k, ref in enumerate(parts):
        start = pl.multiple_of(jnp.bitwise_xor(ints_ref[0], k) * rows, 16)
        up_ref[pl.ds(start, rows)] = ref[:, :columns]
        down_ref[pl.ds(start, rows)] = ref[:, columns:].astype(jnp.float32)


def columns_body(ints_ref, *refs):
    parts, out_ref = refs[:-1], refs[-1]
    columns = parts[0].shape[1]
    for k, ref in enumerate(parts):
        start = pl.multiple_of(jnp.bitwise_xor(ints_ref[0], k) * columns, 128)
        out_ref[:, pl.ds(start, columns)] = ref[...].astype(jnp.float32)


def move_body(scalars_ref, own_ref, w_ref, latents_ref, noise_ref, out_ref):
    velocity = lax.dot_general(
        own_ref[...], w_ref[...], last_axis, preferred_element_type=jnp.float32
    )
    current = latents_ref[...].astype(jnp.float32)
    moved = current - scalars_ref[0] * (
        scalars_ref[1] * velocity + noise_level**2 * current / scalars_ref[2]
    )
    out_ref[...] = (moved + scalars_ref[3] * noise_ref[...].astype(jnp.float32)).astype(
        jnp.bfloat16
    )


def shards(
    latents,
    sampler_noise,
    query_key_value_weight,
    output_weight,
    adapter_down_map,
    adapter_up_map,
    valid_token_count,
    advantage,
    timestep_index,
):
    uly_count = lax.axis_size("uly")
    blk_count = lax.axis_size("blk")
    fsdp_count = lax.axis_size("fsdp")
    uly_id = lax.axis_index("uly")
    blk_id = lax.axis_index("blk")
    uly_int = jnp.reshape(uly_id, (1,)).astype(jnp.int32)
    blk_int = jnp.reshape(blk_id, (1,)).astype(jnp.int32)
    limit = valid_token_count[0]
    rank = adapter_down_map.shape[0]

    rows, width = latents.shape[1:]
    half = rows // 2
    video_slot = lax.axis_index("fsdp") % 4
    moved_a = gather_tokens(latents[0, :half])
    moved_b = gather_tokens(after(latents[0, half:], moved_a))
    work_limit = gather_tokens(jnp.full((8, 128), limit, jnp.int32))[0, 0]

    def norm(x):
        x = x.astype(jnp.float32)
        return (x * lax.rsqrt(jnp.mean(x * x, -1, keepdims=True) + rms_eps)).astype(jnp.bfloat16)

    normed_a, normed_b = norm(moved_a), norm(moved_b)
    heads_here = query_key_value_weight.shape[2] // HEAD_SIZE
    local_columns = heads_here * HEAD_SIZE
    pair = 2 * HEAD_SIZE
    group_rows = uly_count * rows

    weight = pl.pallas_call(
        arrange_body,
        out_shape=jax.ShapeDtypeStruct(
            (query_key_value_weight.shape[1], 3 * local_columns), jnp.bfloat16
        ),
        in_specs=[vmem],
        out_specs=vmem,
        name="arrange",
    )(query_key_value_weight)
    weight_rows = lax.all_gather(weight, "fsdp", axis=0, tiled=True)

    left_a = shift(normed_a, "uly", 1)
    right_a = shift(normed_a, "uly", -1)
    normed_b, relay, _ = lax.optimization_barrier((normed_b, left_a, right_a))
    up = shift(jnp.concatenate((relay, normed_b), 0), "uly", 1)
    right_b = shift(normed_b, "uly", -1)
    far_b = shift(right_b, "uly", -1)

    maps = after(jnp.concatenate((output_weight, adapter_down_map), 0), up, far_b)
    maps = jnp.concatenate([maps] + [exchange(maps, "uly", k) for k in (1, 2, 3)], 1)
    output_columns, down_full = maps[: output_weight.shape[0]], maps[output_weight.shape[0] :]

    def project(first_head, heads):
        return pl.pallas_call(
            project_body,
            out_shape=(
                jax.ShapeDtypeStruct((heads, group_rows, pair), jnp.bfloat16),
                jax.ShapeDtypeStruct((heads, group_rows, HEAD_SIZE), jnp.bfloat16),
            ),
            grid=(heads,),
            in_specs=[smem]
            + [vmem] * 7
            + [pl.BlockSpec((width, local_columns), lambda h: (0, h + first_head))],
            out_specs=(
                pl.BlockSpec((None, group_rows, pair), lambda h: (h, 0, 0)),
                pl.BlockSpec((None, group_rows, HEAD_SIZE), lambda h: (h, 0, 0)),
            ),
            scratch_shapes=[pltpu.VMEM((group_rows, width), jnp.bfloat16)],
            name="project",
        )(uly_int, normed_a, normed_b, left_a, right_a, up, right_b, far_b, weight_rows)

    lead = heads_here - 1
    lead_pairs, lead_queries = project(0, lead)
    last_pairs, last_queries = project(lead, 1)

    key_index = jnp.arange(blk_count * group_rows, dtype=jnp.int32)
    slot = video_slot ^ (key_index // group_rows)
    key_blk = jnp.zeros_like(slot)
    for p in range(blk_count):
        for q in range(4):
            key_blk = jnp.where((blk_id == p) & (slot == q), BLOCK[p][q], key_blk)
    key_pos = (
        (uly_id ^ (key_index % group_rows // rows)) * blk_count
        + key_blk
    ) * rows + key_index % rows
    bias = jnp.where(key_pos < work_limit, 0.0, -1e30).astype(jnp.float32)[None]

    chip_lead = exchange(lead_pairs, "fsdp", 2)
    core_lead = exchange(lead_pairs, "fsdp", 1)
    chip_last = exchange(after(last_pairs, chip_lead), "fsdp", 2)
    core_last = exchange(last_pairs, "fsdp", 1)
    far_lead = exchange(chip_lead, "fsdp", 1)
    far_last = exchange(chip_last, "fsdp", 1)
    weight_full = lax.all_gather(after(output_columns, chip_lead), "fsdp", axis=0, tiled=True)

    segs = attend(lead_queries, (lead_pairs, core_lead, chip_lead, far_lead), bias)
    segs = attend(last_queries, (last_pairs, core_last, chip_last, far_last), bias, segs)
    pieces = [return_tokens(segs[k], k) for k in range(uly_count)]

    step_float = timestep_index[0].astype(jnp.float32)
    time_now = 1.0 - step_float / STEPS
    step_size = 1.0 / STEPS
    noise_std = noise_level * jnp.sqrt(time_now / (1.0 - time_now))
    drift_gain = 1.0 + noise_level**2 / 2.0
    ratio_gain = jnp.sqrt(step_size) * drift_gain / noise_std
    valid_len = limit.astype(jnp.float32)
    ints = jnp.stack([(uly_id * blk_count + blk_id) * rows, limit]).astype(jnp.int32)
    own_heads, narrow_projection, masked, log_tile = pl.pallas_call(
        standard_body,
        out_shape=(
            jax.ShapeDtypeStruct((rows, uly_count * local_columns), jnp.bfloat16),
            jax.ShapeDtypeStruct((rows, rank), jnp.bfloat16),
            jax.ShapeDtypeStruct((rows, width), jnp.bfloat16),
            jax.ShapeDtypeStruct((8, 128), jnp.float32),
        ),
        in_specs=[smem, smem] + [vmem] * (3 + len(pieces)),
        out_specs=(vmem,) * 4,
        name="standard",
    )(ints, jnp.reshape(ratio_gain, (1,)), down_full, adapter_up_map, sampler_noise[0], *pieces)

    up_columns = width // uly_count
    share_columns = up_columns + local_columns
    shares = pl.pallas_call(
        products_body,
        out_shape=[jax.ShapeDtypeStruct((rank, share_columns + 128), jnp.bfloat16)] * uly_count,
        in_specs=[smem] + [vmem] * 5,
        out_specs=[vmem] * uly_count,
        name="products",
    )(uly_int, narrow_projection, masked, adapter_up_map, own_heads, log_tile)

    parts = [shares[0]] + [exchange(shares[k], "uly", k) for k in (1, 2, 3)]
    summed = four_sum([part.astype(jnp.float32) for part in parts])
    part = rank // blk_count

    def rows_of(k):
        return lax.dynamic_slice_in_dim(summed, (blk_id ^ k) * part, part, 0)

    parts = [exchange(rows_of(k), "blk", k) for k in (1, 2, 3)]
    tile = 512
    scalars = jnp.stack(
        [
            jnp.float32(step_size),
            jnp.float32(drift_gain),
            2.0 * (1.0 - time_now),
            noise_std * jnp.sqrt(step_size),
        ]
    )
    token_tile = pl.BlockSpec((rows, tile), lambda i: (0, i))
    next_latents = pl.pallas_call(
        move_body,
        out_shape=jax.ShapeDtypeStruct((rows, width), jnp.bfloat16),
        grid=(width // tile,),
        in_specs=[
            smem,
            pl.BlockSpec(own_heads.shape, lambda i: (0, 0)),
            pl.BlockSpec((tile, own_heads.shape[1]), lambda i: (i, 0)),
            token_tile,
            token_tile,
        ],
        out_specs=token_tile,
        name="move",
    )(scalars, own_heads, weight_full, latents[0], sampler_noise[0])
    next_latents, *parts = lax.optimization_barrier((next_latents, *parts))
    summed = four_sum([rows_of(0)] + parts)
    log_sum = summed[0, share_columns] + summed[0, share_columns + 1] + summed[0, share_columns + 2]
    log_ratio = log_sum / (2.0 * valid_len * width)
    coef = (
        loss_scale
        * advantage[0]
        * jnp.exp(log_ratio)
        * ratio_gain
        / (fsdp_count * valid_len * width)
    )
    summed = summed[:, :share_columns] * coef
    for unit in (4, 1):
        summed = four_sum([summed] + [exchange(summed, "fsdp", unit * k) for k in (1, 2, 3)])

    summed = summed.astype(jnp.bfloat16)
    parts = [exchange(summed, "blk", k) for k in (1, 2, 3)]
    up_mine, grad_down = pl.pallas_call(
        rows_body,
        out_shape=(
            jax.ShapeDtypeStruct((rank, up_columns), jnp.bfloat16),
            jax.ShapeDtypeStruct((rank, local_columns), jnp.float32),
        ),
        in_specs=[smem] + [vmem] * 4,
        out_specs=(vmem,) * 2,
        name="rows",
    )(blk_int, summed, *parts)
    grad_up = pl.pallas_call(
        columns_body,
        out_shape=jax.ShapeDtypeStruct((rank, width), jnp.float32),
        in_specs=[smem] + [vmem] * 4,
        out_specs=vmem,
        name="columns",
    )(uly_int, up_mine, *[exchange(up_mine, "uly", k) for k in (1, 2, 3)])
    return (next_latents[None], jnp.reshape(log_ratio, (1,)), grad_down, grad_up)


def solution(mesh):
    placed = (
        P("fsdp", ("uly", "blk"), None),
        P("fsdp", ("uly", "blk"), None),
        P(None, "fsdp", "uly"),
        P("fsdp", "uly"),
        P(None, "uly"),
        P(),
        P("fsdp"),
        P("fsdp"),
        P(),
    )

    return jax.shard_map(
        shards,
        mesh=mesh,
        in_specs=placed,
        out_specs=(P("fsdp", ("uly", "blk"), None), P("fsdp"), P(None, "uly"), P()),
        check_vma=False,
    )
```

```python
import math

import jax
import jax.numpy as jnp
from jax import lax
from jax.experimental import pallas as pl
from jax.experimental.pallas import tpu as pltpu
from jax.sharding import PartitionSpec as P


HEAD_SIZE = 128
STEPS = 16

noise_level = 0.7
loss_scale = 4194304.0
rms_eps = 1e-06


smem = pl.BlockSpec(memory_space=pltpu.SMEM)
vmem = pl.BlockSpec(memory_space=pltpu.VMEM)
last_axis = (((1,), (1,)), ((), ()))
first_axis = (((0,), (0,)), ((), ()))


PLACE = (0, 2, 1, 3)
SLOT = ((0, 2, 3, 1), (2, 0, 1, 3), (0, 2, 3, 1), (2, 0, 1, 3))
VIDEO = [PLACE.index(p) for p in range(4)]
BLOCK = [[SLOT[VIDEO[p]].index(q) for q in range(4)] for p in range(4)]


def worker(f, b):
    w = f % 4
    return f - w + SLOT[w][b], PLACE[w]


def gather_tokens(x):
    count = lax.axis_size("blk")
    pairs = []
    for f in range(lax.axis_size("fsdp")):
        for b in range(count):
            to_f, to_b = worker(f, b)
            pairs.append((f * count + b, to_f * count + to_b))
    return lax.ppermute(x, ("fsdp", "blk"), pairs)


def return_tokens(x, mask):
    blks, ulys = lax.axis_size("blk"), lax.axis_size("uly")
    pairs = []
    for f in range(lax.axis_size("fsdp")):
        for b in range(blks):
            to_f, to_b = worker(f, b)
            for u in range(ulys):
                pairs.append(
                    ((to_f * ulys + u) * blks + to_b, (f * ulys + (u ^ mask)) * blks + b)
                )
    return lax.ppermute(x, ("fsdp", "uly", "blk"), pairs)


def shift(x, axis, step):
    n = lax.axis_size(axis)
    return lax.ppermute(x, axis, [(i, (i + step) % n) for i in range(n)])


def exchange(x, axis, mask):
    n = lax.axis_size(axis)
    return lax.ppermute(x, axis, [(i, i ^ mask) for i in range(n)])


def after(x, *earlier):
    return lax.optimization_barrier((x,) + earlier)[0]


def four_sum(parts):
    return (parts[0] + parts[1]) + (parts[2] + parts[3])


def arrange_body(w_ref, out_ref):
    at = 0
    for start in range(0, w_ref.shape[2], HEAD_SIZE):
        for j in range(3):
            out_ref[:, at : at + HEAD_SIZE] = w_ref[j, :, start : start + HEAD_SIZE]
            at += HEAD_SIZE


def project_body(
    ints_ref, a_ref, b_ref, left_a_ref, right_a_ref, up_ref, right_b_ref, far_b_ref, w_ref,
    pairs_ref, query_ref, all_ref,
):
    half = a_ref.shape[0]
    rows = 2 * half

    @pl.when(pl.program_id(0) == 0)
    def _():
        odd = lax.rem(ints_ref[0], 2)
        left = pl.multiple_of((3 - 2 * odd) * rows, half)
        right = pl.multiple_of((1 + 2 * odd) * rows, half)
        all_ref[:half] = a_ref[...]
        all_ref[half:rows] = b_ref[...]
        all_ref[pl.ds(left, half)] = left_a_ref[...]
        all_ref[pl.ds(left + half, half)] = up_ref[half:]
        all_ref[pl.ds(right, half)] = right_a_ref[...]
        all_ref[pl.ds(right + half, half)] = right_b_ref[...]
        all_ref[2 * rows : 2 * rows + half] = up_ref[:half]
        all_ref[2 * rows + half : 3 * rows] = far_b_ref[...]

    tile = 384

    def step(r, carry):
        start = pl.multiple_of(r * tile, tile)
        out = jnp.dot(
            all_ref[pl.ds(start, tile)], w_ref[...], preferred_element_type=jnp.float32
        ).astype(jnp.bfloat16)
        query_ref[pl.ds(start, tile)] = out[:, :HEAD_SIZE]
        pairs_ref[pl.ds(start, tile)] = out[:, HEAD_SIZE:]
        return carry

    lax.fori_loop(0, all_ref.shape[0] // tile, step, 0)


def attention_body(q_ref, bias_ref, *refs):
    blocks, earlier = refs[:4], refs[4:-7]
    outs, (pairs_ref, scores_ref, acc_ref) = refs[-7:-3], refs[-3:]
    scale = math.log2(math.e) / math.sqrt(HEAD_SIZE)
    at = 0
    for ref in blocks:
        pairs_ref[at : at + ref.shape[0]] = ref[...]
        at += ref.shape[0]
    chunk = scores_ref.shape[2]
    count = scores_ref.shape[0]
    rows = q_ref.shape[0]

    def score(c, top):
        start = pl.multiple_of(c * chunk, chunk)
        s = lax.dot_general(
            q_ref[...],
            pairs_ref[pl.ds(start, chunk), :HEAD_SIZE],
            last_axis,
            preferred_element_type=jnp.float32,
        )
        s = s + bias_ref[:, pl.ds(start, chunk)]
        scores_ref[c] = s
        for col in range(0, chunk, 128):
            top = jnp.maximum(top, s[:, col : col + 128])
        return top

    top = lax.fori_loop(0, count, score, jnp.full((rows, 128), -jnp.inf, jnp.float32))
    top = jnp.max(top, -1, keepdims=True) * scale
    acc_ref[...] = jnp.zeros_like(acc_ref)

    def collect(c, total):
        start = pl.multiple_of(c * chunk, chunk)
        p = jnp.exp2(scores_ref[c] * scale - top)
        for col in range(0, chunk, 128):
            total = total + p[:, col : col + 128]
        acc_ref[...] += jnp.dot(
            p.astype(jnp.bfloat16),
            pairs_ref[pl.ds(start, chunk), HEAD_SIZE:],
            preferred_element_type=jnp.float32,
        )
        return total

    total = lax.fori_loop(0, count, collect, jnp.zeros((rows, 128), jnp.float32))
    out = (acc_ref[...] / jnp.sum(total, -1, keepdims=True)).astype(jnp.bfloat16)
    seg = rows // len(outs)
    for k, ref in enumerate(outs):
        ref[:, -HEAD_SIZE:] = out[k * seg : (k + 1) * seg]
    for ref, before in zip(outs, earlier):
        ref[:, :-HEAD_SIZE] = before[...]


def attend(queries, blocks, bias, earlier=()):
    heads, rows, _ = queries.shape
    keys = bias.shape[1]
    seg = rows // 4
    columns = heads * HEAD_SIZE + sum(array.shape[1] for array in earlier[:1])
    chunk = 1024

    def spec(array):
        return pl.BlockSpec((None,) + array.shape[1:], lambda i: (i, 0, 0))

    return pl.pallas_call(
        attention_body,
        out_shape=[jax.ShapeDtypeStruct((seg, columns), jnp.bfloat16)] * 4,
        grid=(heads,),
        in_specs=[spec(queries), pl.BlockSpec(bias.shape, lambda i: (0, 0))]
        + [spec(array) for array in blocks]
        + [pl.BlockSpec(array.shape, lambda i: (0, 0)) for array in earlier],
        out_specs=[pl.BlockSpec((seg, columns // heads), lambda i: (0, i))] * 4,
        scratch_shapes=[
            pltpu.VMEM((keys, 2 * HEAD_SIZE), jnp.bfloat16),
            pltpu.VMEM((keys // chunk, rows, chunk), jnp.float32),
            pltpu.VMEM((rows, HEAD_SIZE), jnp.float32),
        ],
        name="attend",
    )(queries, bias, *blocks, *earlier)


def gradients_body(ints_ref, gain_ref, down_ref, up_ref, noise_ref, *refs):
    pieces, own_ref, outs, (narrow_ref, masked_ref) = refs[:4], refs[4], refs[5:-2], refs[-2:]
    rows, width = noise_ref.shape
    at = 0
    for ref in pieces:
        own_ref[:, at : at + ref.shape[1]] = ref[...]
        at += ref.shape[1]
    narrow = lax.dot_general(
        own_ref[...], down_ref[...], last_axis, preferred_element_type=jnp.float32
    ).astype(jnp.bfloat16)
    narrow_ref[...] = narrow
    position = ints_ref[0] + lax.broadcasted_iota(jnp.int32, (rows, 1), 0)
    keep = position < ints_ref[1]
    chunk = 512

    def step(c, total):
        start = pl.multiple_of(c * chunk, chunk)
        change = jnp.dot(
            narrow_ref[...], up_ref[:, pl.ds(start, chunk)], preferred_element_type=jnp.float32
        )
        noise = noise_ref[:, pl.ds(start, chunk)].astype(jnp.float32)
        standard = noise + gain_ref[0] * change
        masked_ref[:, pl.ds(start, chunk)] = jnp.where(keep, standard, 0.0).astype(jnp.bfloat16)
        terms = jnp.where(keep, noise * noise - standard * standard, 0.0)
        for col in range(0, chunk, 128):
            total = total + terms[:, col : col + 128]
        return total

    total = lax.fori_loop(0, width // chunk, step, jnp.zeros((rows, 128), jnp.float32))
    log = jnp.full((outs[0].shape[0], 128), jnp.sum(total))
    column = lax.broadcasted_iota(jnp.int32, log.shape, 1)
    high = log.astype(jnp.bfloat16)
    rest = log - high.astype(jnp.float32)
    middle = rest.astype(jnp.bfloat16)
    low = (rest - middle.astype(jnp.float32)).astype(jnp.bfloat16)
    terms = jnp.where(column == 0, high, jnp.where(column == 1, middle, low))
    count = len(outs)
    columns = width // count
    own_columns = own_ref.shape[1] // count
    low_grad = lax.dot_general(
        masked_ref[...], up_ref[...], last_axis, preferred_element_type=jnp.float32
    ).astype(jnp.bfloat16)
    down = lax.dot_general(
        low_grad, own_ref[...], first_axis, preferred_element_type=jnp.float32
    )
    for k, out in enumerate(outs):
        start = pl.multiple_of(jnp.bitwise_xor(ints_ref[2], k) * columns, 128)
        out[:, :columns] = lax.dot_general(
            narrow_ref[...],
            masked_ref[:, pl.ds(start, columns)],
            first_axis,
            preferred_element_type=jnp.float32,
        ).astype(jnp.bfloat16)
        out[:, columns : columns + own_columns] = down[
            :, k * own_columns : (k + 1) * own_columns
        ].astype(jnp.bfloat16)
        out[:, columns + own_columns :] = terms


def rows_body(ints_ref, *refs):
    parts, up_ref, down_ref = refs[:-2], *refs[-2:]
    rows = parts[0].shape[0]
    columns = up_ref.shape[1]
    for k, ref in enumerate(parts):
        start = pl.multiple_of(jnp.bitwise_xor(ints_ref[0], k) * rows, 16)
        up_ref[pl.ds(start, rows)] = ref[:, :columns]
        down_ref[pl.ds(start, rows)] = ref[:, columns:].astype(jnp.float32)


def columns_body(ints_ref, *refs):
    parts, out_ref = refs[:-1], refs[-1]
    columns = parts[0].shape[1]
    for k, ref in enumerate(parts):
        start = pl.multiple_of(jnp.bitwise_xor(ints_ref[0], k) * columns, 128)
        out_ref[:, pl.ds(start, columns)] = ref[...].astype(jnp.float32)


def move_body(scalars_ref, own_ref, w_ref, latents_ref, noise_ref, out_ref):
    velocity = lax.dot_general(
        own_ref[...], w_ref[...], last_axis, preferred_element_type=jnp.float32
    )
    current = latents_ref[...].astype(jnp.float32)
    moved = current - scalars_ref[0] * (
        scalars_ref[1] * velocity + noise_level**2 * current / scalars_ref[2]
    )
    out_ref[...] = (moved + scalars_ref[3] * noise_ref[...].astype(jnp.float32)).astype(
        jnp.bfloat16
    )


def shards(
    latents,
    sampler_noise,
    query_key_value_weight,
    output_weight,
    adapter_down_map,
    adapter_up_map,
    valid_token_count,
    advantage,
    timestep_index,
):
    uly_count = lax.axis_size("uly")
    blk_count = lax.axis_size("blk")
    fsdp_count = lax.axis_size("fsdp")
    uly_id = lax.axis_index("uly")
    blk_id = lax.axis_index("blk")
    uly_int = jnp.reshape(uly_id, (1,)).astype(jnp.int32)
    blk_int = jnp.reshape(blk_id, (1,)).astype(jnp.int32)
    limit = valid_token_count[0]
    rank = adapter_down_map.shape[0]

    rows, width = latents.shape[1:]
    half = rows // 2
    video_slot = lax.axis_index("fsdp") % 4
    moved_a = gather_tokens(latents[0, :half])
    moved_b = gather_tokens(latents[0, half:])
    work_limit = gather_tokens(jnp.full((8, 128), limit, jnp.int32))[0, 0]

    def norm(x):
        x = x.astype(jnp.float32)
        return (x * lax.rsqrt(jnp.mean(x * x, -1, keepdims=True) + rms_eps)).astype(jnp.bfloat16)

    normed_a, normed_b = norm(moved_a), norm(moved_b)
    heads_here = query_key_value_weight.shape[2] // HEAD_SIZE
    local_columns = heads_here * HEAD_SIZE
    pair = 2 * HEAD_SIZE
    group_rows = uly_count * rows

    weight = pl.pallas_call(
        arrange_body,
        out_shape=jax.ShapeDtypeStruct(
            (query_key_value_weight.shape[1], 3 * local_columns), jnp.bfloat16
        ),
        in_specs=[vmem],
        out_specs=vmem,
        name="arrange",
    )(query_key_value_weight)
    weight_rows = lax.all_gather(weight, "fsdp", axis=0, tiled=True)

    left_a = shift(normed_a, "uly", 1)
    right_a = shift(normed_a, "uly", -1)
    normed_b, relay, _ = lax.optimization_barrier((normed_b, left_a, right_a))
    up = shift(jnp.concatenate((relay, normed_b), 0), "uly", 1)
    right_b = shift(normed_b, "uly", -1)
    far_b = shift(right_b, "uly", -1)

    maps = after(jnp.concatenate((output_weight, adapter_down_map), 0), up, far_b)
    maps = jnp.concatenate([maps] + [exchange(maps, "uly", k) for k in (1, 2, 3)], 1)
    output_columns, down_full = maps[: output_weight.shape[0]], maps[output_weight.shape[0] :]

    def project(first_head, heads):
        return pl.pallas_call(
            project_body,
            out_shape=(
                jax.ShapeDtypeStruct((heads, group_rows, pair), jnp.bfloat16),
                jax.ShapeDtypeStruct((heads, group_rows, HEAD_SIZE), jnp.bfloat16),
            ),
            grid=(heads,),
            in_specs=[smem]
            + [vmem] * 7
            + [pl.BlockSpec((width, local_columns), lambda h: (0, h + first_head))],
            out_specs=(
                pl.BlockSpec((None, group_rows, pair), lambda h: (h, 0, 0)),
                pl.BlockSpec((None, group_rows, HEAD_SIZE), lambda h: (h, 0, 0)),
            ),
            scratch_shapes=[pltpu.VMEM((group_rows, width), jnp.bfloat16)],
            name="project",
        )(uly_int, normed_a, normed_b, left_a, right_a, up, right_b, far_b, weight_rows)

    lead = heads_here - 1
    lead_pairs, lead_queries = project(0, lead)
    last_pairs, last_queries = project(lead, 1)

    key_index = jnp.arange(blk_count * group_rows, dtype=jnp.int32)
    slot = video_slot ^ (key_index // group_rows)
    key_blk = jnp.zeros_like(slot)
    for p in range(blk_count):
        for q in range(4):
            key_blk = jnp.where((blk_id == p) & (slot == q), BLOCK[p][q], key_blk)
    key_pos = (
        (uly_id ^ (key_index % group_rows // rows)) * blk_count
        + key_blk
    ) * rows + key_index % rows
    bias = jnp.where(key_pos < work_limit, 0.0, -1e30).astype(jnp.float32)[None]

    chip_lead = exchange(lead_pairs, "fsdp", 2)
    core_lead = exchange(lead_pairs, "fsdp", 1)
    chip_last = exchange(after(last_pairs, chip_lead), "fsdp", 2)
    core_last = exchange(last_pairs, "fsdp", 1)
    far_lead = exchange(chip_lead, "fsdp", 1)
    far_last = exchange(chip_last, "fsdp", 1)
    weight_full = lax.all_gather(after(output_columns, chip_lead), "fsdp", axis=0, tiled=True)

    segs = attend(lead_queries, (lead_pairs, core_lead, chip_lead, far_lead), bias)
    segs = attend(last_queries, (last_pairs, core_last, chip_last, far_last), bias, segs)
    pieces = [return_tokens(segs[k], k) for k in range(uly_count)]

    step_float = timestep_index[0].astype(jnp.float32)
    time_now = 1.0 - step_float / STEPS
    step_size = 1.0 / STEPS
    noise_std = noise_level * jnp.sqrt(time_now / (1.0 - time_now))
    drift_gain = 1.0 + noise_level**2 / 2.0
    ratio_gain = jnp.sqrt(step_size) * drift_gain / noise_std
    valid_len = limit.astype(jnp.float32)
    ints = jnp.stack([(uly_id * blk_count + blk_id) * rows, limit, uly_id]).astype(jnp.int32)
    up_columns = width // uly_count
    share_columns = up_columns + local_columns
    own_heads, *shares = pl.pallas_call(
        gradients_body,
        out_shape=[jax.ShapeDtypeStruct((rows, uly_count * local_columns), jnp.bfloat16)]
        + [jax.ShapeDtypeStruct((rank, share_columns + 128), jnp.bfloat16)] * uly_count,
        in_specs=[smem, smem] + [vmem] * (3 + len(pieces)),
        out_specs=[vmem] * (1 + uly_count),
        scratch_shapes=[
            pltpu.VMEM((rows, rank), jnp.bfloat16),
            pltpu.VMEM((rows, width), jnp.bfloat16),
        ],
        name="gradients",
    )(ints, jnp.reshape(ratio_gain, (1,)), down_full, adapter_up_map, sampler_noise[0], *pieces)

    parts = [shares[0]] + [exchange(shares[k], "uly", k) for k in (1, 2, 3)]
    summed = four_sum([part.astype(jnp.float32) for part in parts])
    part = rank // blk_count

    def rows_of(k):
        return lax.dynamic_slice_in_dim(summed, (blk_id ^ k) * part, part, 0)

    parts = [exchange(rows_of(k), "blk", k) for k in (1, 2, 3)]
    tile = 512
    scalars = jnp.stack(
        [
            jnp.float32(step_size),
            jnp.float32(drift_gain),
            2.0 * (1.0 - time_now),
            noise_std * jnp.sqrt(step_size),
        ]
    )
    token_tile = pl.BlockSpec((rows, tile), lambda i: (0, i))
    next_latents = pl.pallas_call(
        move_body,
        out_shape=jax.ShapeDtypeStruct((rows, width), jnp.bfloat16),
        grid=(width // tile,),
        in_specs=[
            smem,
            pl.BlockSpec(own_heads.shape, lambda i: (0, 0)),
            pl.BlockSpec((tile, own_heads.shape[1]), lambda i: (i, 0)),
            token_tile,
            token_tile,
        ],
        out_specs=token_tile,
        name="move",
    )(scalars, own_heads, weight_full, latents[0], sampler_noise[0])
    next_latents, *parts = lax.optimization_barrier((next_latents, *parts))
    summed = four_sum([rows_of(0)] + parts)
    log_sum = summed[0, share_columns] + summed[0, share_columns + 1] + summed[0, share_columns + 2]
    log_ratio = log_sum / (2.0 * valid_len * width)
    coef = (
        loss_scale
        * advantage[0]
        * jnp.exp(log_ratio)
        * ratio_gain
        / (fsdp_count * valid_len * width)
    )
    summed = summed[:, :share_columns] * coef
    summed = four_sum([summed] + [exchange(summed, "fsdp", 4 * k) for k in (1, 2, 3)])
    summed = summed + exchange(summed, "fsdp", 1)
    summed = summed + exchange(summed, "fsdp", 2)

    summed = summed.astype(jnp.bfloat16)
    parts = [exchange(summed, "blk", k) for k in (1, 2, 3)]
    up_mine, grad_down = pl.pallas_call(
        rows_body,
        out_shape=(
            jax.ShapeDtypeStruct((rank, up_columns), jnp.bfloat16),
            jax.ShapeDtypeStruct((rank, local_columns), jnp.float32),
        ),
        in_specs=[smem] + [vmem] * 4,
        out_specs=(vmem,) * 2,
        name="rows",
    )(blk_int, summed, *parts)
    grad_up = pl.pallas_call(
        columns_body,
        out_shape=jax.ShapeDtypeStruct((rank, width), jnp.float32),
        in_specs=[smem] + [vmem] * 4,
        out_specs=vmem,
        name="columns",
    )(uly_int, up_mine, *[exchange(up_mine, "uly", k) for k in (1, 2, 3)])
    return (next_latents[None], jnp.reshape(log_ratio, (1,)), grad_down, grad_up)


def solution(mesh):
    placed = (
        P("fsdp", ("uly", "blk"), None),
        P("fsdp", ("uly", "blk"), None),
        P(None, "fsdp", "uly"),
        P("fsdp", "uly"),
        P(None, "uly"),
        P(),
        P("fsdp"),
        P("fsdp"),
        P(),
    )

    return jax.shard_map(
        shards,
        mesh=mesh,
        in_specs=placed,
        out_specs=(P("fsdp", ("uly", "blk"), None), P("fsdp"), P(None, "uly"), P()),
        check_vma=False,
    )
```

```python
import math

import jax
import jax.numpy as jnp
from jax import lax
from jax.experimental import pallas as pl
from jax.experimental.pallas import tpu as pltpu
from jax.sharding import PartitionSpec as P


HEAD_SIZE = 128
STEPS = 16

noise_level = 0.7
loss_scale = 4194304.0
rms_eps = 1e-06


smem = pl.BlockSpec(memory_space=pltpu.SMEM)
vmem = pl.BlockSpec(memory_space=pltpu.VMEM)
last_axis = (((1,), (1,)), ((), ()))
first_axis = (((0,), (0,)), ((), ()))


PLACE = (0, 2, 1, 3)
SLOT = ((0, 2, 3, 1), (2, 0, 1, 3), (0, 2, 3, 1), (2, 0, 1, 3))
VIDEO = [PLACE.index(p) for p in range(4)]
BLOCK = [[SLOT[VIDEO[p]].index(q) for q in range(4)] for p in range(4)]


def worker(f, b):
    w = f % 4
    return f - w + SLOT[w][b], PLACE[w]


def gather_tokens(x):
    count = lax.axis_size("blk")
    pairs = []
    for f in range(lax.axis_size("fsdp")):
        for b in range(count):
            to_f, to_b = worker(f, b)
            pairs.append((f * count + b, to_f * count + to_b))
    return lax.ppermute(x, ("fsdp", "blk"), pairs)


def return_tokens(x, mask):
    blks, ulys = lax.axis_size("blk"), lax.axis_size("uly")
    pairs = []
    for f in range(lax.axis_size("fsdp")):
        for b in range(blks):
            to_f, to_b = worker(f, b)
            for u in range(ulys):
                pairs.append(
                    ((to_f * ulys + u) * blks + to_b, (f * ulys + (u ^ mask)) * blks + b)
                )
    return lax.ppermute(x, ("fsdp", "uly", "blk"), pairs)


def shift(x, axis, step):
    n = lax.axis_size(axis)
    return lax.ppermute(x, axis, [(i, (i + step) % n) for i in range(n)])


def exchange(x, axis, mask):
    n = lax.axis_size(axis)
    return lax.ppermute(x, axis, [(i, i ^ mask) for i in range(n)])


def after(x, *earlier):
    return lax.optimization_barrier((x,) + earlier)[0]


def four_sum(parts):
    return (parts[0] + parts[1]) + (parts[2] + parts[3])


def arrange_body(w_ref, out_ref):
    at = 0
    for start in range(0, w_ref.shape[2], HEAD_SIZE):
        for j in range(3):
            out_ref[:, at : at + HEAD_SIZE] = w_ref[j, :, start : start + HEAD_SIZE]
            at += HEAD_SIZE


def project_body(
    ints_ref, a_ref, b_ref, left_a_ref, right_a_ref, up_ref, right_b_ref, far_b_ref, w_ref,
    pairs_ref, query_ref, all_ref,
):
    half = a_ref.shape[0]
    rows = 2 * half

    @pl.when(pl.program_id(0) == 0)
    def _():
        odd = lax.rem(ints_ref[0], 2)
        left = pl.multiple_of((3 - 2 * odd) * rows, half)
        right = pl.multiple_of((1 + 2 * odd) * rows, half)
        all_ref[:half] = a_ref[...]
        all_ref[half:rows] = b_ref[...]
        all_ref[pl.ds(left, half)] = left_a_ref[...]
        all_ref[pl.ds(left + half, half)] = up_ref[half:]
        all_ref[pl.ds(right, half)] = right_a_ref[...]
        all_ref[pl.ds(right + half, half)] = right_b_ref[...]
        all_ref[2 * rows : 2 * rows + half] = up_ref[:half]
        all_ref[2 * rows + half : 3 * rows] = far_b_ref[...]

    tile = 384

    def step(r, carry):
        start = pl.multiple_of(r * tile, tile)
        out = jnp.dot(
            all_ref[pl.ds(start, tile)], w_ref[...], preferred_element_type=jnp.float32
        ).astype(jnp.bfloat16)
        query_ref[pl.ds(start, tile)] = out[:, :HEAD_SIZE]
        pairs_ref[pl.ds(start, tile)] = out[:, HEAD_SIZE:]
        return carry

    lax.fori_loop(0, all_ref.shape[0] // tile, step, 0)


def attention_body(q_ref, bias_ref, *refs):
    blocks, earlier = refs[:4], refs[4:-7]
    outs, (pairs_ref, scores_ref, acc_ref) = refs[-7:-3], refs[-3:]
    scale = math.log2(math.e) / math.sqrt(HEAD_SIZE)
    at = 0
    for ref in blocks:
        pairs_ref[at : at + ref.shape[0]] = ref[...]
        at += ref.shape[0]
    chunk = scores_ref.shape[2]
    count = scores_ref.shape[0]
    rows = q_ref.shape[0]

    def score(c, top):
        start = pl.multiple_of(c * chunk, chunk)
        s = lax.dot_general(
            q_ref[...],
            pairs_ref[pl.ds(start, chunk), :HEAD_SIZE],
            last_axis,
            preferred_element_type=jnp.float32,
        )
        s = s + bias_ref[:, pl.ds(start, chunk)]
        scores_ref[c] = s
        for col in range(0, chunk, 128):
            top = jnp.maximum(top, s[:, col : col + 128])
        return top

    top = lax.fori_loop(0, count, score, jnp.full((rows, 128), -jnp.inf, jnp.float32))
    top = jnp.max(top, -1, keepdims=True) * scale
    acc_ref[...] = jnp.zeros_like(acc_ref)

    def collect(c, total):
        start = pl.multiple_of(c * chunk, chunk)
        p = jnp.exp2(scores_ref[c] * scale - top)
        for col in range(0, chunk, 128):
            total = total + p[:, col : col + 128]
        acc_ref[...] += jnp.dot(
            p.astype(jnp.bfloat16),
            pairs_ref[pl.ds(start, chunk), HEAD_SIZE:],
            preferred_element_type=jnp.float32,
        )
        return total

    total = lax.fori_loop(0, count, collect, jnp.zeros((rows, 128), jnp.float32))
    out = (acc_ref[...] / jnp.sum(total, -1, keepdims=True)).astype(jnp.bfloat16)
    seg = rows // len(outs)
    for k, ref in enumerate(outs):
        ref[:, -HEAD_SIZE:] = out[k * seg : (k + 1) * seg]
    for ref, before in zip(outs, earlier):
        ref[:, :-HEAD_SIZE] = before[...]


def attend(queries, blocks, bias, earlier=()):
    heads, rows, _ = queries.shape
    keys = bias.shape[1]
    seg = rows // 4
    columns = heads * HEAD_SIZE + sum(array.shape[1] for array in earlier[:1])
    chunk = 1024

    def spec(array):
        return pl.BlockSpec((None,) + array.shape[1:], lambda i: (i, 0, 0))

    return pl.pallas_call(
        attention_body,
        out_shape=[jax.ShapeDtypeStruct((seg, columns), jnp.bfloat16)] * 4,
        grid=(heads,),
        in_specs=[spec(queries), pl.BlockSpec(bias.shape, lambda i: (0, 0))]
        + [spec(array) for array in blocks]
        + [pl.BlockSpec(array.shape, lambda i: (0, 0)) for array in earlier],
        out_specs=[pl.BlockSpec((seg, columns // heads), lambda i: (0, i))] * 4,
        scratch_shapes=[
            pltpu.VMEM((keys, 2 * HEAD_SIZE), jnp.bfloat16),
            pltpu.VMEM((keys // chunk, rows, chunk), jnp.float32),
            pltpu.VMEM((rows, HEAD_SIZE), jnp.float32),
        ],
        name="attend",
    )(queries, bias, *blocks, *earlier)


def gradients_body(ints_ref, gain_ref, down_ref, up_ref, noise_ref, *refs):
    pieces, own_ref, outs, (narrow_ref, masked_ref) = refs[:4], refs[4], refs[5:-2], refs[-2:]
    rows, width = noise_ref.shape
    at = 0
    for ref in pieces:
        own_ref[:, at : at + ref.shape[1]] = ref[...]
        at += ref.shape[1]
    narrow = lax.dot_general(
        own_ref[...], down_ref[...], last_axis, preferred_element_type=jnp.float32
    ).astype(jnp.bfloat16)
    narrow_ref[...] = narrow
    position = ints_ref[0] + lax.broadcasted_iota(jnp.int32, (rows, 1), 0)
    keep = position < ints_ref[1]
    chunk = 512

    def step(c, total):
        start = pl.multiple_of(c * chunk, chunk)
        change = jnp.dot(
            narrow_ref[...], up_ref[:, pl.ds(start, chunk)], preferred_element_type=jnp.float32
        )
        noise = noise_ref[:, pl.ds(start, chunk)].astype(jnp.float32)
        standard = noise + gain_ref[0] * change
        masked_ref[:, pl.ds(start, chunk)] = jnp.where(keep, standard, 0.0).astype(jnp.bfloat16)
        terms = jnp.where(keep, noise * noise - standard * standard, 0.0)
        for col in range(0, chunk, 128):
            total = total + terms[:, col : col + 128]
        return total

    total = lax.fori_loop(0, width // chunk, step, jnp.zeros((rows, 128), jnp.float32))
    log = jnp.full((outs[0].shape[0], 128), jnp.sum(total))
    column = lax.broadcasted_iota(jnp.int32, log.shape, 1)
    high = log.astype(jnp.bfloat16)
    rest = log - high.astype(jnp.float32)
    middle = rest.astype(jnp.bfloat16)
    low = (rest - middle.astype(jnp.float32)).astype(jnp.bfloat16)
    terms = jnp.where(column == 0, high, jnp.where(column == 1, middle, low))
    count = len(outs)
    columns = width // count
    own_columns = own_ref.shape[1] // count
    low_grad = lax.dot_general(
        masked_ref[...], up_ref[...], last_axis, preferred_element_type=jnp.float32
    ).astype(jnp.bfloat16)
    down = lax.dot_general(
        low_grad, own_ref[...], first_axis, preferred_element_type=jnp.float32
    )
    for k, out in enumerate(outs):
        start = pl.multiple_of(jnp.bitwise_xor(ints_ref[2], k) * columns, 128)
        out[:, :columns] = lax.dot_general(
            narrow_ref[...],
            masked_ref[:, pl.ds(start, columns)],
            first_axis,
            preferred_element_type=jnp.float32,
        ).astype(jnp.bfloat16)
        out[:, columns : columns + own_columns] = down[
            :, k * own_columns : (k + 1) * own_columns
        ].astype(jnp.bfloat16)
        out[:, columns + own_columns :] = terms


def rows_body(ints_ref, *refs):
    parts, up_ref, down_ref = refs[:-2], *refs[-2:]
    rows = parts[0].shape[0]
    columns = up_ref.shape[1]
    for k, ref in enumerate(parts):
        start = pl.multiple_of(jnp.bitwise_xor(ints_ref[0], k) * rows, 16)
        up_ref[pl.ds(start, rows)] = ref[:, :columns]
        down_ref[pl.ds(start, rows)] = ref[:, columns:].astype(jnp.float32)


def columns_body(ints_ref, *refs):
    parts, out_ref = refs[:-1], refs[-1]
    columns = parts[0].shape[1]
    for k, ref in enumerate(parts):
        start = pl.multiple_of(jnp.bitwise_xor(ints_ref[0], k) * columns, 128)
        out_ref[:, pl.ds(start, columns)] = ref[...].astype(jnp.float32)


def move_body(scalars_ref, own_ref, w_ref, latents_ref, noise_ref, out_ref):
    velocity = lax.dot_general(
        own_ref[...], w_ref[...], last_axis, preferred_element_type=jnp.float32
    )
    current = latents_ref[...].astype(jnp.float32)
    moved = current - scalars_ref[0] * (
        scalars_ref[1] * velocity + noise_level**2 * current / scalars_ref[2]
    )
    out_ref[...] = (moved + scalars_ref[3] * noise_ref[...].astype(jnp.float32)).astype(
        jnp.bfloat16
    )


def shards(
    latents,
    sampler_noise,
    query_key_value_weight,
    output_weight,
    adapter_down_map,
    adapter_up_map,
    valid_token_count,
    advantage,
    timestep_index,
):
    uly_count = lax.axis_size("uly")
    blk_count = lax.axis_size("blk")
    fsdp_count = lax.axis_size("fsdp")
    uly_id = lax.axis_index("uly")
    blk_id = lax.axis_index("blk")
    uly_int = jnp.reshape(uly_id, (1,)).astype(jnp.int32)
    blk_int = jnp.reshape(blk_id, (1,)).astype(jnp.int32)
    limit = valid_token_count[0]
    rank = adapter_down_map.shape[0]

    rows, width = latents.shape[1:]
    half = rows // 2
    video_slot = lax.axis_index("fsdp") % 4
    moved_a = gather_tokens(latents[0, :half])
    moved_b = gather_tokens(latents[0, half:])
    work_limit = gather_tokens(jnp.full((8, 128), limit, jnp.int32))[0, 0]

    def norm(x):
        x = x.astype(jnp.float32)
        return (x * lax.rsqrt(jnp.mean(x * x, -1, keepdims=True) + rms_eps)).astype(jnp.bfloat16)

    normed_a, normed_b = norm(moved_a), norm(moved_b)
    heads_here = query_key_value_weight.shape[2] // HEAD_SIZE
    local_columns = heads_here * HEAD_SIZE
    pair = 2 * HEAD_SIZE
    group_rows = uly_count * rows

    weight = pl.pallas_call(
        arrange_body,
        out_shape=jax.ShapeDtypeStruct(
            (query_key_value_weight.shape[1], 3 * local_columns), jnp.bfloat16
        ),
        in_specs=[vmem],
        out_specs=vmem,
        name="arrange",
    )(query_key_value_weight)
    weight_rows = lax.all_gather(weight, "fsdp", axis=0, tiled=True)

    left_a = shift(normed_a, "uly", 1)
    right_a = shift(normed_a, "uly", -1)
    normed_b, relay, _ = lax.optimization_barrier((normed_b, left_a, right_a))
    up = shift(jnp.concatenate((relay, normed_b), 0), "uly", 1)
    right_b = shift(normed_b, "uly", -1)
    far_b = shift(right_b, "uly", -1)

    maps = after(jnp.concatenate((output_weight, adapter_down_map), 0), up, far_b)
    maps = [maps] + [exchange(maps, "uly", k) for k in (1, 2, 3)]
    mine = output_weight.shape[0]
    output_columns = jnp.concatenate([m[:mine] for m in maps], 1)
    down_full = jnp.concatenate([m[mine:] for m in maps], 1)

    def project(first_head, heads):
        return pl.pallas_call(
            project_body,
            out_shape=(
                jax.ShapeDtypeStruct((heads, group_rows, pair), jnp.bfloat16),
                jax.ShapeDtypeStruct((heads, group_rows, HEAD_SIZE), jnp.bfloat16),
            ),
            grid=(heads,),
            in_specs=[smem]
            + [vmem] * 7
            + [pl.BlockSpec((width, local_columns), lambda h: (0, h + first_head))],
            out_specs=(
                pl.BlockSpec((None, group_rows, pair), lambda h: (h, 0, 0)),
                pl.BlockSpec((None, group_rows, HEAD_SIZE), lambda h: (h, 0, 0)),
            ),
            scratch_shapes=[pltpu.VMEM((group_rows, width), jnp.bfloat16)],
            name="project",
        )(uly_int, normed_a, normed_b, left_a, right_a, up, right_b, far_b, weight_rows)

    lead = heads_here - 1
    lead_pairs, lead_queries = project(0, lead)
    last_pairs, last_queries = project(lead, 1)

    key_index = jnp.arange(blk_count * group_rows, dtype=jnp.int32)
    slot = video_slot ^ (key_index // group_rows)
    key_blk = jnp.zeros_like(slot)
    for p in range(blk_count):
        for q in range(4):
            key_blk = jnp.where((blk_id == p) & (slot == q), BLOCK[p][q], key_blk)
    key_pos = (
        (uly_id ^ (key_index % group_rows // rows)) * blk_count
        + key_blk
    ) * rows + key_index % rows
    bias = jnp.where(key_pos < work_limit, 0.0, -1e30).astype(jnp.float32)[None]

    chip_lead = exchange(lead_pairs, "fsdp", 2)
    core_lead = exchange(lead_pairs, "fsdp", 1)
    chip_last = exchange(after(last_pairs, chip_lead), "fsdp", 2)
    core_last = exchange(last_pairs, "fsdp", 1)
    far_lead = exchange(chip_lead, "fsdp", 1)
    far_last = exchange(chip_last, "fsdp", 1)
    weight_full = lax.all_gather(after(output_columns, chip_lead), "fsdp", axis=0, tiled=True)

    segs = attend(lead_queries, (lead_pairs, core_lead, chip_lead, far_lead), bias)
    segs = attend(last_queries, (last_pairs, core_last, chip_last, far_last), bias, segs)
    pieces = [return_tokens(segs[k], k) for k in range(uly_count)]

    step_float = timestep_index[0].astype(jnp.float32)
    time_now = 1.0 - step_float / STEPS
    step_size = 1.0 / STEPS
    noise_std = noise_level * jnp.sqrt(time_now / (1.0 - time_now))
    drift_gain = 1.0 + noise_level**2 / 2.0
    ratio_gain = jnp.sqrt(step_size) * drift_gain / noise_std
    valid_len = limit.astype(jnp.float32)
    ints = jnp.stack([(uly_id * blk_count + blk_id) * rows, limit, uly_id]).astype(jnp.int32)
    up_columns = width // uly_count
    share_columns = up_columns + local_columns
    own_heads, *shares = pl.pallas_call(
        gradients_body,
        out_shape=[jax.ShapeDtypeStruct((rows, uly_count * local_columns), jnp.bfloat16)]
        + [jax.ShapeDtypeStruct((rank, share_columns + 128), jnp.bfloat16)] * uly_count,
        in_specs=[smem, smem] + [vmem] * (3 + len(pieces)),
        out_specs=[vmem] * (1 + uly_count),
        scratch_shapes=[
            pltpu.VMEM((rows, rank), jnp.bfloat16),
            pltpu.VMEM((rows, width), jnp.bfloat16),
        ],
        name="gradients",
    )(ints, jnp.reshape(ratio_gain, (1,)), down_full, adapter_up_map, sampler_noise[0], *pieces)

    parts = [shares[0]] + [exchange(shares[k], "uly", k) for k in (1, 2, 3)]
    summed = four_sum([part.astype(jnp.float32) for part in parts])
    part = rank // blk_count

    def rows_of(k):
        return lax.dynamic_slice_in_dim(summed, (blk_id ^ k) * part, part, 0)

    parts = [exchange(rows_of(k), "blk", k) for k in (1, 2, 3)]
    tile = 768
    scalars = jnp.stack(
        [
            jnp.float32(step_size),
            jnp.float32(drift_gain),
            2.0 * (1.0 - time_now),
            noise_std * jnp.sqrt(step_size),
        ]
    )
    token_tile = pl.BlockSpec((rows, tile), lambda i: (0, i))
    next_latents = pl.pallas_call(
        move_body,
        out_shape=jax.ShapeDtypeStruct((rows, width), jnp.bfloat16),
        grid=(width // tile,),
        in_specs=[
            smem,
            pl.BlockSpec(own_heads.shape, lambda i: (0, 0)),
            pl.BlockSpec((tile, own_heads.shape[1]), lambda i: (i, 0)),
            token_tile,
            token_tile,
        ],
        out_specs=token_tile,
        name="move",
    )(scalars, own_heads, weight_full, latents[0], sampler_noise[0])
    next_latents, *parts = lax.optimization_barrier((next_latents, *parts))
    summed = four_sum([rows_of(0)] + parts)
    log_sum = summed[0, share_columns] + summed[0, share_columns + 1] + summed[0, share_columns + 2]
    log_ratio = log_sum / (2.0 * valid_len * width)
    coef = (
        loss_scale
        * advantage[0]
        * jnp.exp(log_ratio)
        * ratio_gain
        / (fsdp_count * valid_len * width)
    )
    summed = summed[:, :share_columns] * coef
    summed = four_sum([summed] + [exchange(summed, "fsdp", 4 * k) for k in (1, 2, 3)])
    summed = summed + exchange(summed, "fsdp", 1)
    summed = summed + exchange(summed, "fsdp", 2)

    summed = summed.astype(jnp.bfloat16)
    parts = [exchange(summed, "blk", k) for k in (1, 2, 3)]
    up_mine, grad_down = pl.pallas_call(
        rows_body,
        out_shape=(
            jax.ShapeDtypeStruct((rank, up_columns), jnp.bfloat16),
            jax.ShapeDtypeStruct((rank, local_columns), jnp.float32),
        ),
        in_specs=[smem] + [vmem] * 4,
        out_specs=(vmem,) * 2,
        name="rows",
    )(blk_int, summed, *parts)
    grad_up = pl.pallas_call(
        columns_body,
        out_shape=jax.ShapeDtypeStruct((rank, width), jnp.float32),
        in_specs=[smem] + [vmem] * 4,
        out_specs=vmem,
        name="columns",
    )(uly_int, up_mine, *[exchange(up_mine, "uly", k) for k in (1, 2, 3)])
    return (next_latents[None], jnp.reshape(log_ratio, (1,)), grad_down, grad_up)


def solution(mesh):
    placed = (
        P("fsdp", ("uly", "blk"), None),
        P("fsdp", ("uly", "blk"), None),
        P(None, "fsdp", "uly"),
        P("fsdp", "uly"),
        P(None, "uly"),
        P(),
        P("fsdp"),
        P("fsdp"),
        P(),
    )

    return jax.shard_map(
        shards,
        mesh=mesh,
        in_specs=placed,
        out_specs=(P("fsdp", ("uly", "blk"), None), P("fsdp"), P(None, "uly"), P()),
        check_vma=False,
    )
```
